32 devices in a mesh: tm: 16 (over z, y, x), mp: 2 (over core).
Axes of the slice: x: 2, y: 2, z: 4, core: 2. Of those that a mesh axis runs over, the one named last changes fastest.
Arguments:
- queries: bfloat16 [4096, 1536], P('tm', 'mp'), may hold values from -300 to 300
- upstream: bfloat16 [4096, 1536], P('tm', 'mp'), may hold values from -180 to 180
- bounds: int32 [4096, 2], P('tm'), may hold values from 0 to 12288, as said below
- frame_keys: bfloat16 [12288, 1536], P('tm', 'mp'), may hold values from -6 to 6
- frame_values: bfloat16 [12288, 1536], P('tm', 'mp'), may hold values from -6 to 6
- hidden_pre: bfloat16 [12288, 3072], P('tm', 'mp'), may hold values from -9 to 9
- expand_weight: bfloat16 [1536, 3072], P(None, 'mp'), may hold values from -0.15625 to 0.15625
- shrink_weight: bfloat16 [3072, 1536], P('mp'), may hold values from -0.109375 to 0.109375
- key_weight: bfloat16 [1536, 1536], P(None, 'mp'), may hold values from -0.15625 to 0.15625
- value_weight: bfloat16 [1536, 1536], P(None, 'mp'), may hold values from -0.15625 to 0.15625
- kernel_taps: bfloat16 [31, 1536], P(None, 'mp'), may hold values from -1.1953125 to 1.1953125
Outputs:
- frame_gradient: bfloat16 [12288, 1536], P('tm', 'mp')
- query_gradient: bfloat16 [4096, 1536], P('tm', 'mp')
The draws below stay inside these ranges and needn't reach their ends.
Inputs may be any that keep to these rules, and one draw needn't show every extreme that they name: `bounds`: row t holds a token's start (column 0) and end (column 1). With s = t // 256: (s - 1) * 768 <= start < end <= (s + 2) * 768 and end - start <= 768; in every draw some token has start = (s - 1) * 768, some token has end = (s + 2) * 768, and some token has end - start = 768.
All inputs are finite; a program needn't handle non-finite values.
Results may differ from the reference program's by a relative error of at most 0.019.
Values may be sent and summed in bfloat16 or wider, within the bound.
A program may use at most 128 MiB of HBM per device.

```python
import math
import jax
import jax.numpy as jnp
from jax import lax

HEADS = 16
HD = 96
D = 1536
FF = 3072
KERNEL = 31
HALF = 15
T_DEV = 256
F_DEV = 768
TOKENS = 4096
FRAMES = 12288
N_TM = 16
N_MP = 2


def window_parts(key):
    base = jax.random.fold_in(key, 4409)
    streams = jax.random.split(base, 6)
    shards = TOKENS // T_DEV
    ratio = FRAMES // TOKENS
    tokens_at = jnp.arange(TOKENS, dtype=jnp.int32)
    shard_of = tokens_at // T_DEV
    within = tokens_at - shard_of * T_DEV
    rates = jax.random.randint(streams[0], (shards,), 1, 2 * ratio)
    offsets = jax.random.randint(streams[1], (shards,), -(F_DEV // 2), F_DEV // 2)
    jitter = jax.random.randint(streams[2], (TOKENS,), 0, ratio)
    center = shard_of * F_DEV + offsets[shard_of] + within * rates[shard_of] + jitter
    center = jnp.clip(center, shard_of * F_DEV - F_DEV // 2, (shard_of + 1) * F_DEV + F_DEV // 2 - 1)
    center = jnp.clip(center, 0, FRAMES - 1)
    spans = jax.random.randint(streams[3], (TOKENS,), max(2, F_DEV // 16), F_DEV + 1)
    starts = jnp.maximum(center - spans // 2, 0)
    stops = jnp.minimum(starts + spans, FRAMES)
    first = jax.random.randint(streams[4], (), 1, shards) * T_DEV
    first_start = (first // T_DEV - 1) * F_DEV
    starts = starts.at[first].set(first_start)
    stops = stops.at[first].set(first_start + F_DEV)
    last = jax.random.randint(streams[5], (), 0, shards - 1) * T_DEV + T_DEV - 1
    last_stop = (last // T_DEV + 2) * F_DEV
    stops = stops.at[last].set(last_stop)
    starts = starts.at[last].set(last_stop - F_DEV)
    return jnp.stack([starts, stops], 1).astype(jnp.int32)


def key_parts(key):
    base = jax.random.fold_in(key, 5521)
    streams = jax.random.split(base, 1)
    drawn = jax.random.truncated_normal(streams[0], -6.0, 6.0, (FRAMES, D), jnp.float32)
    return drawn


def draw_bounds(key, part):
    return window_parts(key)


def draw_frame_keys(key, part):
    return key_parts(key).astype(jnp.bfloat16)


def draw_queries(key, part):
    base = jax.random.fold_in(key, 6637)
    rows = jax.random.truncated_normal(base, -6.0, 6.0, (TOKENS, D), jnp.float32)
    return rows.astype(jnp.bfloat16)


def shard_levels(stream_key, shape, cuts, least, largest):
    level, own = 1.0, jax.random.fold_in(stream_key, 6)
    for axis_at, shards_of in cuts:
        steps = jnp.exp(jax.random.uniform(jax.random.fold_in(own, axis_at), (shards_of,), jnp.float32, least / len(cuts), largest / len(cuts)))
        level = level * jnp.repeat(steps, shape[axis_at] // shards_of).reshape([-1 if axis == axis_at else 1 for axis in range(len(shape))])
    return level


def scatter_about(rng, dims, scale, most, cuts=(), held_as=jnp.bfloat16):
    values = scale * jax.random.normal(rng, dims, jnp.float32)
    if cuts:
        values = values * shard_levels(rng, dims, cuts, -0.22, 0.18)
    return jnp.clip(values, -most, most).astype(held_as)


def setup_inputs(seed: int = 0) -> dict:
    streams_of = jax.random.split(jax.random.key(seed), 12)
    return {
        "queries": draw_queries(jax.random.fold_in(streams_of[11], 71), 0),
        "upstream": scatter_about(streams_of[1], (TOKENS, D), 30.0, 180.0, ((0, 16), (1, 2))),
        "bounds": draw_bounds(jax.random.fold_in(streams_of[11], 71), 0),
        "frame_keys": draw_frame_keys(jax.random.fold_in(streams_of[11], 71), 0),
        "frame_values": scatter_about(streams_of[4], (FRAMES, D), 1.0, 6.0, ((0, 16), (1, 2))),
        "hidden_pre": scatter_about(streams_of[5], (FRAMES, FF), 1.5, 9.0, ((0, 16), (1, 2))),
        "expand_weight": scatter_about(streams_of[6], (D, FF), D ** -0.5, 0.15625, ((1, 2),)),
        "shrink_weight": scatter_about(streams_of[7], (FF, D), FF ** -0.5, 0.109375, ((0, 2),)),
        "key_weight": scatter_about(streams_of[8], (D, D), D ** -0.5, 0.15625, ((1, 2),)),
        "value_weight": scatter_about(streams_of[9], (D, D), D ** -0.5, 0.15625, ((1, 2),)),
        "kernel_taps": scatter_about(streams_of[10], (KERNEL, D), 0.2, 1.1953125, ((1, 2),)),
    }


masked_fill = -1e+30

def round_trip(values):
    return lax.optimization_barrier(values.astype(jnp.bfloat16)).astype(jnp.float32)

def silu_slope(hidden_pre):
    logistic = jax.nn.sigmoid(hidden_pre)
    return logistic * (1.0 + hidden_pre * (1.0 - logistic))

def reference(queries, upstream, bounds, frame_keys, frame_values, hidden_pre, expand_weight, shrink_weight, key_weight, value_weight, kernel_taps):
    score_scale = 1.0 / math.sqrt(HD)
    highest = lax.Precision.HIGHEST
    padding = jnp.zeros((F_DEV, D), frame_keys.dtype)
    keys_padded = jnp.concatenate([padding, frame_keys, padding], 0)
    values_padded = jnp.concatenate([padding, frame_values, padding], 0)

    def shard_step(carry, shard_index):
        key_acc, value_acc = carry
        query_rows = lax.dynamic_slice_in_dim(queries, shard_index * T_DEV, T_DEV, 0).astype(jnp.float32).reshape(T_DEV, HEADS, HD)
        upstream_rows = lax.dynamic_slice_in_dim(upstream, shard_index * T_DEV, T_DEV, 0).astype(jnp.float32).reshape(T_DEV, HEADS, HD)
        bound_rows = lax.dynamic_slice_in_dim(bounds, shard_index * T_DEV, T_DEV, 0)
        frame_start = shard_index * F_DEV
        keys_near = lax.dynamic_slice_in_dim(keys_padded, frame_start, 3 * F_DEV, 0).astype(jnp.float32).reshape(3 * F_DEV, HEADS, HD)
        values_near = lax.dynamic_slice_in_dim(values_padded, frame_start, 3 * F_DEV, 0).astype(jnp.float32).reshape(3 * F_DEV, HEADS, HD)
        positions = (shard_index - 1) * F_DEV + jnp.arange(3 * F_DEV, dtype=jnp.int32)
        inside = (positions[None, :] >= bound_rows[:, 0:1]) & (positions[None, :] < bound_rows[:, 1:2])
        inside = inside[None]
        scores = jnp.einsum('thd,fhd->htf', query_rows, keys_near, precision=highest) * score_scale
        row_max = lax.optimization_barrier(jnp.max(jnp.where(inside, scores, masked_fill), -1, keepdims=True))
        row_sum = lax.optimization_barrier(jnp.sum(jnp.where(inside, jnp.exp(scores - row_max), 0.0), -1, keepdims=True))
        log_total = row_max + jnp.log(row_sum)
        probabilities = jnp.where(inside, jnp.exp(scores - log_total), 0.0)
        slopes = jnp.einsum('thd,fhd->htf', upstream_rows, values_near, precision=highest)
        row_delta = lax.optimization_barrier(jnp.sum(probabilities * slopes, -1, keepdims=True))
        score_gradient = round_trip(probabilities * (slopes - row_delta) * score_scale)
        probs_low = round_trip(probabilities)
        query_part = jnp.einsum('htf,fhd->thd', score_gradient, keys_near, precision=highest).reshape(T_DEV, D).astype(jnp.bfloat16)
        key_part = jnp.einsum('htf,thd->fhd', score_gradient, query_rows, precision=highest).reshape(3 * F_DEV, D)
        value_part = jnp.einsum('htf,thd->fhd', probs_low, upstream_rows, precision=highest).reshape(3 * F_DEV, D)
        key_acc = lax.dynamic_update_slice_in_dim(key_acc, lax.dynamic_slice_in_dim(key_acc, frame_start, 3 * F_DEV, 0) + key_part, frame_start, 0)
        value_acc = lax.dynamic_update_slice_in_dim(value_acc, lax.dynamic_slice_in_dim(value_acc, frame_start, 3 * F_DEV, 0) + value_part, frame_start, 0)
        return ((key_acc, value_acc), query_part)
    zeros = jnp.zeros((FRAMES + 2 * F_DEV, D), jnp.float32)
    (key_acc, value_acc), query_parts = lax.scan(shard_step, (zeros, zeros), jnp.arange(N_TM, dtype=jnp.int32))
    query_gradient = query_parts.reshape(TOKENS, D)
    key_low = key_acc[F_DEV:F_DEV + FRAMES].astype(jnp.bfloat16)
    value_low = value_acc[F_DEV:F_DEV + FRAMES].astype(jnp.bfloat16)
    group_width = D // N_MP
    encoder_sum = jnp.zeros((FRAMES, D), jnp.float32)
    for group in range(N_MP):
        lower = group * group_width
        upper = lower + group_width
        term = jnp.dot(key_low[:, lower:upper], key_weight[:, lower:upper].T, preferred_element_type=jnp.float32)
        term = term + jnp.dot(value_low[:, lower:upper], value_weight[:, lower:upper].T, preferred_element_type=jnp.float32)
        encoder_sum = encoder_sum + round_trip(term)
    encoder_low = encoder_sum.astype(jnp.bfloat16)
    act_gradient = 0.5 * jnp.dot(encoder_low, shrink_weight.T, preferred_element_type=jnp.float32)
    pre_gradient = (act_gradient * silu_slope(hidden_pre.astype(jnp.float32))).astype(jnp.bfloat16)
    unit_width = FF // N_MP
    hidden_back = jnp.zeros((FRAMES, D), jnp.float32)
    for group in range(N_MP):
        lower = group * unit_width
        upper = lower + unit_width
        term = jnp.dot(pre_gradient[:, lower:upper], expand_weight[:, lower:upper].T, preferred_element_type=jnp.float32)
        hidden_back = hidden_back + round_trip(term)
    hidden_gradient = round_trip(encoder_sum + hidden_back)
    padded = jnp.pad(hidden_gradient, ((HALF, HALF), (0, 0)))
    weights = kernel_taps.astype(jnp.float32)
    result = hidden_gradient
    for tap_index in range(KERNEL):
        lower = 2 * HALF - tap_index
        result = result + weights[tap_index] * padded[lower:lower + FRAMES]
    return (result.astype(jnp.bfloat16), query_gradient)
```

```python
import functools
import math

import jax
import jax.numpy as jnp
from jax import lax
from jax.experimental import pallas as pl
from jax.experimental.pallas import tpu as pltpu
from jax.sharding import PartitionSpec as P

HD = 96
KERNEL = 31
HALF = 15
LANES = 128
HALO = 16
masked_fill = -1e30
VMEM = pl.BlockSpec(memory_space=pltpu.VMEM)


def shifted(value, axis, by):
    peers = lax.axis_size(axis)
    pairs = [(i, i + by) for i in range(peers) if 0 <= i + by < peers]
    return lax.ppermute(value, axis, pairs)


def contract_last(left, right):
    return lax.dot_general(
        left, right, (((1,), (1,)), ((), ())), preferred_element_type=jnp.float32
    )


def mm(left, right):
    return jnp.dot(left, right, preferred_element_type=jnp.float32)


def silu_slope(hidden_pre):
    logistic = jax.nn.sigmoid(hidden_pre)
    return logistic * (1.0 + hidden_pre * (1.0 - logistic))


def window_of(width):
    return min(2 * LANES, width)


def window_start(pair):
    return 384 * (pair // 2) + LANES * (pair % 2)


def mask_heads(src_ref, dst_ref):
    heads, _, window = dst_ref.shape
    column = lax.broadcasted_iota(jnp.int32, (1, window), 1)
    for head in range(heads):
        low = window_start(head // 2)
        at = head * HD - low
        keep = jnp.where((column >= at) & (column < at + HD), 1.0, 0.0).astype(jnp.bfloat16)
        dst_ref[head] = src_ref[:, low : low + window] * keep


def frame_tiles(bounds_ref, bias_ref, offset, tile, body):
    frames, tokens = bias_ref.shape
    begin = bounds_ref[0:1, :] + offset
    end = bounds_ref[1:2, :] + offset
    for index in range(frames // tile):
        low = index * tile
        touch = (begin < low + tile) & (end > low)
        active = jnp.max(jnp.where(touch, 1.0, 0.0)) > 0.0

        @pl.when(active)
        def _():
            row = low + lax.broadcasted_iota(jnp.int32, (tile, tokens), 0)
            inside = (row >= begin) & (row < end)
            bias_ref[low : low + tile, :] = jnp.where(inside, 0.0, masked_fill)
            body(low)


def stats_kernel(offsets, tile, scale, k_ref, v_ref, *refs):
    guests = len(offsets)
    inputs, outputs = refs[: 3 * guests], refs[3 * guests : 4 * guests]
    qm_ref, um_ref, bias_ref = refs[4 * guests :]
    heads, tokens, window = qm_ref.shape
    for guest, offset in enumerate(offsets):
        q_ref, u_ref, b_ref = inputs[3 * guest : 3 * guest + 3]
        out = outputs[guest]
        mask_heads(q_ref, qm_ref)
        mask_heads(u_ref, um_ref)
        out[0:heads, :] = jnp.full((heads, tokens), masked_fill, jnp.float32)
        out[heads:, :] = jnp.zeros((2 * heads, tokens), jnp.float32)

        def body(low):
            def pair_step(pair, carry):
                cols = pl.ds(pl.multiple_of(window_start(pair), LANES), window)
                keys = k_ref[low : low + tile, cols]
                values = v_ref[low : low + tile, cols]
                bias = bias_ref[low : low + tile, :]
                for side in range(2):
                    head = 2 * pair + side
                    scores = contract_last(keys, qm_ref[head]) + bias
                    slopes = contract_last(values, um_ref[head])
                    old = out[pl.ds(head, 1), :]
                    new = jnp.maximum(old, jnp.max(scores, 0, keepdims=True))
                    fade = jnp.exp((old - new) * scale)
                    expos = jnp.exp((scores - new) * scale)
                    out[pl.ds(head, 1), :] = new
                    out[pl.ds(heads + head, 1), :] = out[
                        pl.ds(heads + head, 1), :
                    ] * fade + jnp.sum(expos, 0, keepdims=True)
                    out[pl.ds(2 * heads + head, 1), :] = out[
                        pl.ds(2 * heads + head, 1), :
                    ] * fade + jnp.sum(expos * slopes, 0, keepdims=True)
                return carry

            lax.fori_loop(0, heads // 2, pair_step, 0)

        frame_tiles(b_ref, bias_ref, offset, tile, body)


def grads_kernel(offsets, tile, scale, n_stats, final, k_ref, v_ref, kt_ref, *refs):
    guests = len(offsets)
    per = 3 + n_stats
    inputs, refs = refs[: per * guests], refs[per * guests :]
    if final:
        dk_in, dv_in, dk_out, dv_out, dq_out = refs[:5]
        dq_outs = [dq_out]
        qm_ref, um_ref, bias_ref, norm_ref, dqt_ref, dk_ref, dv_ref = refs[5:]
        dk_ref[...] = dk_in[...]
        dv_ref[...] = dv_in[...]
    else:
        dk_ref, dv_ref = refs[:2]
        dq_outs = refs[2 : 2 + guests]
        qm_ref, um_ref, bias_ref, norm_ref, dqt_ref = refs[2 + guests :]
        dk_ref[...] = jnp.zeros_like(dk_ref)
        dv_ref[...] = jnp.zeros_like(dv_ref)
    heads, tokens, window = qm_ref.shape
    for guest, offset in enumerate(offsets):
        q_ref, u_ref, b_ref = inputs[per * guest : per * guest + 3]
        stats = [r[...] for r in inputs[per * guest + 3 : per * guest + per]]
        peak = stats[0][0:heads]
        for one in stats[1:]:
            peak = jnp.maximum(peak, one[0:heads])
        total = jnp.zeros_like(peak)
        weighted = jnp.zeros_like(peak)
        for one in stats:
            factor = jnp.exp((one[0:heads] - peak) * scale)
            total = total + one[heads : 2 * heads] * factor
            weighted = weighted + one[2 * heads :] * factor
        total = jnp.where(total > 0.0, total, 1.0)
        norm_ref[0:heads, :] = peak * scale + jnp.log(total)
        norm_ref[heads:, :] = weighted / total
        mask_heads(q_ref, qm_ref)
        mask_heads(u_ref, um_ref)
        dqt_ref[...] = jnp.zeros_like(dqt_ref)

        def body(low):
            def pair_step(pair, carry):
                cols = pl.ds(pl.multiple_of(window_start(pair), LANES), window)
                keys = k_ref[low : low + tile, cols]
                values = v_ref[low : low + tile, cols]
                inside = bias_ref[low : low + tile, :] == 0.0
                key_term = value_term = None
                for side in range(2):
                    head = 2 * pair + side
                    scores = contract_last(keys, qm_ref[head])
                    slopes = contract_last(values, um_ref[head])
                    log_total = norm_ref[pl.ds(head, 1), :]
                    delta = norm_ref[pl.ds(heads + head, 1), :]
                    probs = jnp.where(inside, jnp.exp(scores * scale - log_total), 0.0)
                    grad = (probs * ((slopes - delta) * scale)).astype(jnp.bfloat16)
                    key_one = mm(grad, qm_ref[head])
                    value_one = mm(probs.astype(jnp.bfloat16), um_ref[head])
                    key_term = key_one if side == 0 else key_term + key_one
                    value_term = value_one if side == 0 else value_term + value_one
                    rows = pl.ds(pl.multiple_of(head * HD, HD // 3), HD)
                    dqt_ref[rows, :] += mm(kt_ref[rows, low : low + tile], grad)
                dk_ref[low : low + tile, cols] += key_term
                dv_ref[low : low + tile, cols] += value_term
                return carry

            lax.fori_loop(0, heads // 2, pair_step, 0)

        frame_tiles(b_ref, bias_ref, offset, tile, body)
        dq_outs[guest][...] = dqt_ref[...].T.astype(dq_outs[guest].dtype)
    if final:
        dk_out[...] = dk_ref[...].astype(jnp.bfloat16)
        dv_out[...] = dv_ref[...].astype(jnp.bfloat16)


def conv_kernel(block, h_ref, before_ref, after_ref, taps_ref, out_ref, x_ref, w_ref):
    chunks, rows, _ = x_ref.shape
    frames = rows - 2 * HALO
    for chunk in range(chunks):
        cols = slice(chunk * LANES, (chunk + 1) * LANES)
        x_ref[chunk, 0:HALO, :] = before_ref[:, cols].astype(jnp.float32)
        x_ref[chunk, HALO : HALO + frames, :] = h_ref[:, cols].astype(jnp.float32)
        x_ref[chunk, HALO + frames :, :] = after_ref[:, cols].astype(jnp.float32)
        w_ref[chunk, 0:KERNEL, :] = taps_ref[:, cols].astype(jnp.float32)
    for chunk in range(chunks):
        cols = slice(chunk * LANES, (chunk + 1) * LANES)

        def step(index, carry):
            low = pl.multiple_of(index * block, block)
            acc = x_ref[chunk, pl.ds(low + HALO, block), :]
            for tap in range(KERNEL):
                acc = acc + w_ref[chunk, tap : tap + 1, :] * x_ref[
                    chunk, pl.ds(low + HALO + HALF - tap, block), :
                ]
            out_ref[pl.ds(low, block), cols] = acc.astype(jnp.bfloat16)
            return carry

        lax.fori_loop(0, frames // block, step, 0)


def tile_of(frames):
    for tile in (256, 128, 64, 32, 16):
        if frames % tile == 0:
            return tile
    return frames


def params(mib=None):
    return pltpu.CompilerParams(vmem_limit_bytes=None if mib is None else mib << 20)


def attention(queries, upstream, bounds, frame_keys, frame_values):
    frames, width = frame_keys.shape
    tokens = queries.shape[0]
    heads = width // HD
    window = window_of(width)
    scale = 1.0 / math.sqrt(HD)
    tile = tile_of(frames)
    base = lax.axis_index("tm") * frames
    local = (bounds - base).T
    f32, bf16 = jnp.float32, jnp.bfloat16
    own = (queries, upstream, local)
    prev = tuple(shifted(x, "tm", 1) for x in own)
    after = tuple(shifted(x, "tm", -1) for x in own)
    keys_t = frame_keys.T
    shape = jax.ShapeDtypeStruct
    masks = [
        pltpu.VMEM((heads, tokens, window), bf16),
        pltpu.VMEM((heads, tokens, window), bf16),
        pltpu.VMEM((frames, tokens), f32),
    ]
    stat = shape((3 * heads, tokens), f32)
    work = 2 * tokens * frames * width

    def stats(offsets, guests):
        out = pl.pallas_call(
            functools.partial(stats_kernel, offsets, tile, scale),
            out_shape=[stat] * len(offsets),
            in_specs=[VMEM] * (2 + 3 * len(offsets)),
            out_specs=[VMEM] * len(offsets),
            scratch_shapes=masks,
            compiler_params=params(24),
            cost_estimate=pl.CostEstimate(
                flops=5 * work * len(offsets), bytes_accessed=4 * frames * width, transcendentals=0
            ),
            name="stats%d" % len(offsets),
        )(frame_keys, frame_values, *[x for guest in guests for x in guest])
        return list(out)

    (own_stats,) = stats((0,), (own,))
    prev_own = shifted(own_stats, "tm", 1)
    after_own = shifted(own_stats, "tm", -1)
    prev_stats, after_stats = stats((-frames, frames), (prev, after))
    from_after = shifted(prev_stats, "tm", -1)
    from_prev = shifted(after_stats, "tm", 1)
    position = lax.axis_index("tm")
    last = lax.axis_size("tm") - 1
    empty = jnp.where(jnp.arange(3 * heads) < heads, masked_fill, 0.0).astype(f32)[:, None]
    from_prev = jnp.where(position == 0, empty, from_prev)
    from_after = jnp.where(position == last, empty, from_after)

    grad_scratch = [
        pltpu.VMEM((2 * heads, tokens), f32),
        pltpu.VMEM((width, tokens), f32),
    ]
    accs = [pltpu.VMEM((frames, width), f32)] * 2
    dk, dv, prev_dq, after_dq = pl.pallas_call(
        functools.partial(grads_kernel, (-frames, frames), tile, scale, 2, False),
        out_shape=[shape((frames, width), f32)] * 2 + [shape((tokens, width), bf16)] * 2,
        in_specs=[VMEM] * 13,
        out_specs=[VMEM] * 4,
        scratch_shapes=masks + grad_scratch,
        compiler_params=params(32),
        cost_estimate=pl.CostEstimate(
            flops=20 * work, bytes_accessed=20 * frames * width, transcendentals=0
        ),
        name="grads2",
    )(frame_keys, frame_values, keys_t, *prev, prev_stats, prev_own, *after, after_stats, after_own)
    back_prev = shifted(prev_dq, "tm", -1)
    back_after = shifted(after_dq, "tm", 1)
    key_low, value_low, own_dq = pl.pallas_call(
        functools.partial(grads_kernel, (0,), tile, scale, 3, True),
        out_shape=[shape((frames, width), bf16)] * 2 + [shape((tokens, width), f32)],
        in_specs=[VMEM] * 11,
        out_specs=[VMEM] * 3,
        scratch_shapes=masks + grad_scratch + accs,
        compiler_params=params(40),
        cost_estimate=pl.CostEstimate(
            flops=10 * work, bytes_accessed=20 * frames * width, transcendentals=0
        ),
        name="grads1",
    )(frame_keys, frame_values, keys_t, *own, own_stats, from_prev, from_after, dk, dv)
    query_gradient = own_dq + back_prev.astype(f32) + back_after.astype(f32)
    return key_low, value_low, query_gradient.astype(bf16)


def depthwise(hidden_gradient, kernel_taps):
    frames, width = hidden_gradient.shape
    before = shifted(hidden_gradient[frames - HALO :], "tm", 1)
    after = shifted(hidden_gradient[:HALO], "tm", -1)
    chunks = width // LANES
    return pl.pallas_call(
        functools.partial(conv_kernel, tile_of(frames) // 4),
        out_shape=jax.ShapeDtypeStruct((frames, width), jnp.bfloat16),
        in_specs=[VMEM] * 4,
        out_specs=VMEM,
        scratch_shapes=[
            pltpu.VMEM((chunks, frames + 2 * HALO, LANES), jnp.float32),
            pltpu.VMEM((chunks, KERNEL + 1, LANES), jnp.float32),
        ],
        compiler_params=params(16),
        name="conv",
    )(hidden_gradient, before, after, kernel_taps)


def plain_depthwise(hidden_gradient, kernel_taps):
    frames = hidden_gradient.shape[0]
    before = shifted(hidden_gradient[frames - HALF :], "tm", 1)
    after = shifted(hidden_gradient[:HALF], "tm", -1)
    padded = jnp.concatenate([before, hidden_gradient, after], 0).astype(jnp.float32)
    weights = kernel_taps.astype(jnp.float32)
    result = hidden_gradient.astype(jnp.float32)
    for tap in range(KERNEL):
        lower = 2 * HALF - tap
        result = result + weights[tap] * padded[lower : lower + frames]
    return result.astype(jnp.bfloat16)


def mp_sum(part):
    if lax.axis_size("mp") == 2:
        other = lax.ppermute(part, "mp", [(0, 1), (1, 0)])
        return part.astype(jnp.float32) + other.astype(jnp.float32)
    return lax.psum(part, "mp").astype(jnp.float32)


def mp_scatter(part, width):
    me = lax.axis_index("mp")
    if lax.axis_size("mp") == 2:
        mine = lax.dynamic_slice_in_dim(part, me * width, width, 1)
        theirs = lax.dynamic_slice_in_dim(part, (1 - me) * width, width, 1)
        other = lax.ppermute(theirs, "mp", [(0, 1), (1, 0)])
        return mine.astype(jnp.float32) + other.astype(jnp.float32)
    return lax.psum_scatter(part, "mp", scatter_dimension=1, tiled=True).astype(jnp.float32)


def feed_forward(key_low, value_low, hidden_pre, expand_weight, shrink_weight, key_weight, value_weight):
    frames, width = key_low.shape
    pieces = 2 if frames % 32 == 0 else 1
    size = frames // pieces
    me = lax.axis_index("mp")
    sums = []
    for piece in range(pieces):
        rows = slice(piece * size, (piece + 1) * size)
        part = contract_last(key_low[rows], key_weight) + contract_last(value_low[rows], value_weight)
        sums.append(mp_sum(part.astype(jnp.bfloat16)))
    out = []
    for piece in range(pieces):
        rows = slice(piece * size, (piece + 1) * size)
        act = 0.5 * contract_last(sums[piece].astype(jnp.bfloat16), shrink_weight)
        pre = (act * silu_slope(hidden_pre[rows].astype(jnp.float32))).astype(jnp.bfloat16)
        back = mp_scatter(contract_last(pre, expand_weight).astype(jnp.bfloat16), width)
        mine = lax.dynamic_slice_in_dim(sums[piece], me * width, width, 1)
        out.append((mine + back).astype(jnp.bfloat16))
    return jnp.concatenate(out, 0) if pieces > 1 else out[0]


def shards(
    queries,
    upstream,
    bounds,
    frame_keys,
    frame_values,
    hidden_pre,
    expand_weight,
    shrink_weight,
    key_weight,
    value_weight,
    kernel_taps,
):
    key_low, value_low, query_gradient = attention(
        queries, upstream, bounds, frame_keys, frame_values
    )
    hidden_gradient = feed_forward(
        key_low, value_low, hidden_pre, expand_weight, shrink_weight, key_weight, value_weight
    )
    if hidden_gradient.shape[1] % LANES == 0:
        frame_gradient = depthwise(hidden_gradient, kernel_taps)
    else:
        frame_gradient = plain_depthwise(hidden_gradient, kernel_taps)
    return (frame_gradient, query_gradient)


def solution(mesh):
    placed = (
        P("tm", "mp"),
        P("tm", "mp"),
        P("tm", None),
        P("tm", "mp"),
        P("tm", "mp"),
        P("tm", "mp"),
        P(None, "mp"),
        P("mp", None),
        P(None, "mp"),
        P(None, "mp"),
        P(None, "mp"),
    )
    return jax.shard_map(
        shards,
        mesh=mesh,
        in_specs=placed,
        out_specs=(P("tm", "mp"), P("tm", "mp")),
        check_vma=False,
    )
```

```python
import functools
import math

import jax
import jax.numpy as jnp
from jax import lax
from jax.experimental import pallas as pl
from jax.experimental.pallas import tpu as pltpu
from jax.sharding import PartitionSpec as P

HD = 96
KERNEL = 31
HALF = 15
LANES = 128
HALO = 16
masked_fill = -1e30
VMEM = pl.BlockSpec(memory_space=pltpu.VMEM)


def shifted(value, axis, by):
    peers = lax.axis_size(axis)
    pairs = [(i, i + by) for i in range(peers) if 0 <= i + by < peers]
    return lax.ppermute(value, axis, pairs)


def contract_last(left, right):
    return lax.dot_general(
        left, right, (((1,), (1,)), ((), ())), preferred_element_type=jnp.float32
    )


def mm(left, right):
    return jnp.dot(left, right, preferred_element_type=jnp.float32)


def silu_slope(hidden_pre):
    logistic = jax.nn.sigmoid(hidden_pre)
    return logistic * (1.0 + hidden_pre * (1.0 - logistic))


def window_of(width):
    return min(2 * LANES, width)


def window_start(pair):
    return 384 * (pair // 2) + LANES * (pair % 2)


def mask_heads(src_ref, dst_ref):
    heads, _, window = dst_ref.shape
    column = lax.broadcasted_iota(jnp.int32, (1, window), 1)
    for head in range(heads):
        low = window_start(head // 2)
        at = head * HD - low
        keep = jnp.where((column >= at) & (column < at + HD), 1.0, 0.0).astype(jnp.bfloat16)
        dst_ref[head] = src_ref[:, low : low + window] * keep


def frame_tiles(bounds_ref, bias_ref, offset, tile, body):
    frames, tokens = bias_ref.shape
    begin = bounds_ref[0:1, :] + offset
    end = bounds_ref[1:2, :] + offset
    for index in range(frames // tile):
        low = index * tile
        touch = (begin < low + tile) & (end > low)
        active = jnp.max(jnp.where(touch, 1.0, 0.0)) > 0.0

        @pl.when(active)
        def _():
            row = low + lax.broadcasted_iota(jnp.int32, (tile, tokens), 0)
            inside = (row >= begin) & (row < end)
            bias_ref[low : low + tile, :] = jnp.where(inside, 0.0, masked_fill)
            body(low)


def stats_kernel(offsets, tile, scale, k_ref, v_ref, *refs):
    guests = len(offsets)
    inputs, outputs = refs[: 3 * guests], refs[3 * guests : 4 * guests]
    qm_ref, um_ref, bias_ref = refs[4 * guests :]
    heads, tokens, window = qm_ref.shape
    for guest, offset in enumerate(offsets):
        q_ref, u_ref, b_ref = inputs[3 * guest : 3 * guest + 3]
        out = outputs[guest]
        mask_heads(q_ref, qm_ref)
        mask_heads(u_ref, um_ref)
        out[0:heads, :] = jnp.full((heads, tokens), masked_fill, jnp.float32)
        out[heads:, :] = jnp.zeros((2 * heads, tokens), jnp.float32)

        def body(low):
            def pair_step(pair, carry):
                cols = pl.ds(pl.multiple_of(window_start(pair), LANES), window)
                keys = k_ref[low : low + tile, cols]
                values = v_ref[low : low + tile, cols]
                bias = bias_ref[low : low + tile, :]
                for side in range(2):
                    head = 2 * pair + side
                    scores = contract_last(keys, qm_ref[head]) + bias
                    slopes = contract_last(values, um_ref[head])
                    old = out[pl.ds(head, 1), :]
                    new = jnp.maximum(old, jnp.max(scores, 0, keepdims=True))
                    fade = jnp.exp((old - new) * scale)
                    expos = jnp.exp((scores - new) * scale)
                    out[pl.ds(head, 1), :] = new
                    out[pl.ds(heads + head, 1), :] = out[
                        pl.ds(heads + head, 1), :
                    ] * fade + jnp.sum(expos, 0, keepdims=True)
                    out[pl.ds(2 * heads + head, 1), :] = out[
                        pl.ds(2 * heads + head, 1), :
                    ] * fade + jnp.sum(expos * slopes, 0, keepdims=True)
                return carry

            lax.fori_loop(0, heads // 2, pair_step, 0)

        frame_tiles(b_ref, bias_ref, offset, tile, body)


def bias_from(bounds_ref, bias_ref, tile):
    frames, tokens = bias_ref.shape
    begin, end = bounds_ref[0:1, :], bounds_ref[1:2, :]

    def step(index, carry):
        low = pl.multiple_of(index * tile, tile)
        row = low + lax.broadcasted_iota(jnp.int32, (tile, tokens), 0)
        inside = (row >= begin) & (row < end)
        bias_ref[pl.ds(low, tile), :] = jnp.where(inside, 0.0, masked_fill)
        return carry

    lax.fori_loop(0, frames // tile, step, 0)


def pair_stats(pair, tile, scale, k_ref, v_ref, q, u, bias_ref, out, qm_ref, um_ref):
    frames, tokens = bias_ref.shape
    _, _, window = qm_ref.shape
    heads = out.shape[0] // 3
    low = window_start(pair)
    cols = slice(low, low + window)
    column = lax.broadcasted_iota(jnp.int32, (1, window), 1)
    for side in range(2):
        at = (2 * pair + side) * HD - low
        keep = jnp.where((column >= at) & (column < at + HD), 1.0, 0.0).astype(jnp.bfloat16)
        qm_ref[side] = q[:, cols] * keep
        um_ref[side] = u[:, cols] * keep

    def step(index, carry):
        rows = pl.ds(pl.multiple_of(index * tile, tile), tile)
        keys, values = k_ref[rows, cols], v_ref[rows, cols]
        bias = bias_ref[rows, :]
        result = []
        for side in range(2):
            old, total, weighted = carry[3 * side : 3 * side + 3]
            scores = contract_last(keys, qm_ref[side]) + bias
            slopes = contract_last(values, um_ref[side])
            new = jnp.maximum(old, jnp.max(scores, 0, keepdims=True))
            fade = jnp.exp((old - new) * scale)
            expos = jnp.exp((scores - new) * scale)
            result += [
                new,
                total * fade + jnp.sum(expos, 0, keepdims=True),
                weighted * fade + jnp.sum(expos * slopes, 0, keepdims=True),
            ]
        return tuple(result)

    zero = jnp.zeros((1, tokens), jnp.float32)
    start = (zero + masked_fill, zero, zero)
    done = lax.fori_loop(0, frames // tile, step, start + start)
    for side in range(2):
        head = 2 * pair + side
        for kind in range(3):
            out[kind * heads + head : kind * heads + head + 1, :] = done[3 * side + kind]


def exchange_kernel(
    tile, scale, q_ref, u_ref, b_ref, k_ref, v_ref,
    near, far, rel, own_ref, here_ref, peer_ref, back_ref,
    transit, b_near, b_far, bias_ref, qm_ref, um_ref, send, recv_near, recv_y, recv_far,
    stat_send, stat_recv, b_send, b_recv,
):
    me = lax.axis_index("tm")
    count = lax.axis_size("tm")
    frames = k_ref.shape[0]
    heads = own_ref.shape[0] // 3
    place = lax.rem(me, 4)
    odd = lax.rem(me, 2)
    x_peer = me + 1 - 2 * odd
    y_peer = jnp.where(place < 2, me + 2, me - 2)
    far_peer = me - 1 + 2 * odd
    has_far = (far_peer >= 0) & (far_peer < count)
    corner = (place == 0) | (place == 3)
    up = jnp.where(place == 0, me + 4, me - 4)
    down = jnp.where(place == 0, me - 4, me + 4)
    has_up = corner & (up >= 0) & (up < count)
    has_down = corner & (down >= 0) & (down < count)

    barrier = pltpu.get_barrier_semaphore()

    def greet(peer):
        pl.semaphore_signal(
            barrier, inc=1, device_id={"tm": peer}, device_id_type=pl.DeviceIdType.MESH
        )

    greet(x_peer)
    greet(y_peer)
    pl.when(has_far)(lambda: greet(far_peer))
    pl.when(has_up)(lambda: greet(up))
    pl.when(has_down)(lambda: greet(down))
    callers = 2
    for there in (has_far, has_up, has_down):
        callers = callers + jnp.where(there, 1, 0)
    pl.semaphore_wait(barrier, callers)

    def remote(src, dst, send_sem, recv_sem, peer):
        return pltpu.make_async_remote_copy(
            src_ref=src, dst_ref=dst, send_sem=send_sem, recv_sem=recv_sem,
            device_id={"tm": peer}, device_id_type=pl.DeviceIdType.MESH,
        )

    steps = 2 * (q_ref.shape[1] // LANES)

    def part(c):
        return slice((c // 2) * LANES, (c // 2 + 1) * LANES)

    def first(c):
        src = q_ref if c % 2 == 0 else u_ref
        return remote(
            src.at[:, part(c)], near.at[c % 2, :, part(c)], send.at[0, c], recv_near.at[c], x_peer
        )

    def second_final(c):
        return remote(
            near.at[c % 2, :, part(c)], far.at[c % 2, :, part(c)], send.at[1, c], recv_far.at[c], y_peer
        )

    def second_transit(c):
        return remote(
            near.at[c % 2, :, part(c)], transit.at[c % 2, :, part(c)], send.at[1, c], recv_y.at[c], y_peer
        )

    def third(c):
        return remote(
            transit.at[c % 2, :, part(c)], far.at[c % 2, :, part(c)], send.at[2, c], recv_far.at[c], up
        )

    to_near = remote(b_ref, b_near, b_send.at[0], b_recv.at[0], x_peer)
    to_far = remote(b_ref, b_far, b_send.at[1], b_recv.at[1], far_peer)
    to_near.start()
    pl.when(has_far)(lambda: to_far.start())
    for c in range(steps):
        first(c).start()

    @pl.when(jnp.logical_not(has_far))
    def _():
        far[...] = jnp.zeros_like(far)
        b_far[...] = jnp.zeros_like(b_far)
        peer_ref[1] = jnp.zeros_like(own_ref)
        back_ref[1, 0:heads, :] = jnp.full((heads, own_ref.shape[1]), masked_fill, jnp.float32)
        back_ref[1, heads:, :] = jnp.zeros((2 * heads, own_ref.shape[1]), jnp.float32)

    base = me * frames
    rel[0] = b_ref[...] - base
    bias_from(rel.at[0], bias_ref.at[0], tile)

    own_sends = [
        remote(own_ref, peer_ref.at[0], stat_send.at[0], stat_recv.at[0], x_peer),
        remote(own_ref, peer_ref.at[1], stat_send.at[1], stat_recv.at[1], far_peer),
    ]
    back_sends = [
        remote(here_ref.at[0], back_ref.at[0], stat_send.at[2], stat_recv.at[2], x_peer),
        remote(here_ref.at[1], back_ref.at[1], stat_send.at[3], stat_recv.at[3], far_peer),
    ]

    def own_unit(pair):
        pair_stats(pair, tile, scale, k_ref, v_ref, q_ref, u_ref, bias_ref.at[0], own_ref, qm_ref, um_ref)
        if pair == heads // 2 - 1:
            own_sends[0].start()
            pl.when(has_far)(lambda: own_sends[1].start())

    def near_unit(pair):
        pair_stats(
            pair, tile, scale, k_ref, v_ref, near.at[0], near.at[1], bias_ref.at[1], here_ref.at[0], qm_ref, um_ref
        )
        if pair == heads // 2 - 1:
            back_sends[0].start()

    def far_unit(pair):
        pair_stats(
            pair, tile, scale, k_ref, v_ref, far.at[0], far.at[1], bias_ref.at[2], here_ref.at[1], qm_ref, um_ref
        )

    def need(pair):
        return 2 * ((window_start(pair) + 2 * LANES) // LANES)

    waited_far = [0]
    passed_y = [0]

    def pass_on(upto):
        while passed_y[0] < upto:
            c = passed_y[0]

            @pl.when(corner)
            def _():
                second_transit(c).wait_recv()
                pl.when(has_up)(lambda: third(c).start())

            passed_y[0] += 1

    def far_ready(upto):
        while waited_far[0] < upto:
            c = waited_far[0]
            pl.when(has_far)(lambda: second_final(c).wait_recv())
            waited_far[0] += 1

    pairs = heads // 2
    near_next, own_next, far_next = 0, 0, 0
    for c in range(steps):
        first(c).wait_recv()
        pl.when(corner)(lambda: second_final(c).start())
        pl.when(jnp.logical_not(corner))(lambda: second_transit(c).start())
        pass_on(c - 1)
        if c == 0:
            to_near.wait_recv()
            rel[1] = b_near[...] - base
            bias_from(rel.at[1], bias_ref.at[1], tile)
        if own_next < pairs:
            own_unit(own_next)
            own_next += 1
        elif near_next < pairs and need(near_next) <= c + 1:
            near_unit(near_next)
            near_next += 1
        elif far_next < pairs and need(far_next) <= c - 3:
            if far_next == 0:
                pl.when(has_far)(lambda: to_far.wait_recv())
                rel[2] = b_far[...] - base
                bias_from(rel.at[2], bias_ref.at[2], tile)
            far_ready(need(far_next))
            far_unit(far_next)
            far_next += 1
    while passed_y[0] < steps or near_next < pairs or far_next < pairs:
        pass_on(min(steps, passed_y[0] + 1 if passed_y[0] < steps - 2 else steps))
        if near_next < pairs:
            near_unit(near_next)
            near_next += 1
            continue
        if far_next < pairs:
            if far_next == 0:
                pl.when(has_far)(lambda: to_far.wait_recv())
                rel[2] = b_far[...] - base
                bias_from(rel.at[2], bias_ref.at[2], tile)
            if need(far_next) > steps - 4:
                pass_on(steps)
            far_ready(need(far_next))
            far_unit(far_next)
            far_next += 1
    far_ready(steps)
    pl.when(has_far)(lambda: back_sends[1].start())

    to_near.wait_send()
    pl.when(has_far)(lambda: to_far.wait_send())
    for c in range(steps):
        first(c).wait_send()
        second_final(c).wait_send()
        pl.when(has_up)(lambda: third(c).wait_send())
    own_sends[0].wait()
    back_sends[0].wait()

    @pl.when(has_far)
    def _():
        own_sends[1].wait()
        back_sends[1].wait()


def grads_kernel(offsets, n_stats, tile, scale, k_ref, v_ref, kt_ref, *refs):
    guests = len(offsets)
    inputs = []
    for kinds in n_stats:
        inputs.append(refs[: 3 + kinds])
        refs = refs[3 + kinds :]
    dk_out, dv_out = refs[:2]
    dq_outs = refs[2 : 2 + guests]
    qm_ref, um_ref, bias_ref, norm_ref, dqt_ref, dk_ref, dv_ref = refs[2 + guests :]
    dk_ref[...] = jnp.zeros_like(dk_ref)
    dv_ref[...] = jnp.zeros_like(dv_ref)
    heads, tokens, window = qm_ref.shape
    for guest, offset in enumerate(offsets):
        q_ref, u_ref, b_ref = inputs[guest][:3]
        stats = [r[...] for r in inputs[guest][3:]]
        peak = stats[0][0:heads]
        for one in stats[1:]:
            peak = jnp.maximum(peak, one[0:heads])
        total = jnp.zeros_like(peak)
        weighted = jnp.zeros_like(peak)
        for one in stats:
            factor = jnp.exp((one[0:heads] - peak) * scale)
            total = total + one[heads : 2 * heads] * factor
            weighted = weighted + one[2 * heads :] * factor
        total = jnp.where(total > 0.0, total, 1.0)
        norm_ref[0:heads, :] = peak * scale + jnp.log(total)
        norm_ref[heads:, :] = weighted / total
        mask_heads(q_ref, qm_ref)
        mask_heads(u_ref, um_ref)
        dqt_ref[...] = jnp.zeros_like(dqt_ref)

        def body(low):
            def pair_step(pair, carry):
                cols = pl.ds(pl.multiple_of(window_start(pair), LANES), window)
                keys = k_ref[low : low + tile, cols]
                values = v_ref[low : low + tile, cols]
                inside = bias_ref[low : low + tile, :] == 0.0
                key_term = value_term = None
                for side in range(2):
                    head = 2 * pair + side
                    scores = contract_last(keys, qm_ref[head])
                    slopes = contract_last(values, um_ref[head])
                    log_total = norm_ref[pl.ds(head, 1), :]
                    delta = norm_ref[pl.ds(heads + head, 1), :]
                    probs = jnp.where(inside, jnp.exp(scores * scale - log_total), 0.0)
                    grad = (probs * ((slopes - delta) * scale)).astype(jnp.bfloat16)
                    key_one = mm(grad, qm_ref[head])
                    value_one = mm(probs.astype(jnp.bfloat16), um_ref[head])
                    key_term = key_one if side == 0 else key_term + key_one
                    value_term = value_one if side == 0 else value_term + value_one
                    rows = pl.ds(pl.multiple_of(head * HD, HD // 3), HD)
                    dqt_ref[rows, :] += mm(kt_ref[rows, low : low + tile], grad)
                dk_ref[low : low + tile, cols] += key_term
                dv_ref[low : low + tile, cols] += value_term
                return carry

            lax.fori_loop(0, heads // 2, pair_step, 0)

        frame_tiles(b_ref, bias_ref, offset, tile, body)
        dq_outs[guest][...] = dqt_ref[...].T.astype(dq_outs[guest].dtype)
    dk_out[...] = dk_ref[...].astype(jnp.bfloat16)
    dv_out[...] = dv_ref[...].astype(jnp.bfloat16)


def conv_kernel(block, h_ref, before_ref, after_ref, taps_ref, out_ref, x_ref, w_ref):
    chunks, rows, _ = x_ref.shape
    frames = rows - 2 * HALO
    for chunk in range(chunks):
        cols = slice(chunk * LANES, (chunk + 1) * LANES)
        x_ref[chunk, 0:HALO, :] = before_ref[:, cols].astype(jnp.float32)
        x_ref[chunk, HALO : HALO + frames, :] = h_ref[:, cols].astype(jnp.float32)
        x_ref[chunk, HALO + frames :, :] = after_ref[:, cols].astype(jnp.float32)
        w_ref[chunk, 0:KERNEL, :] = taps_ref[:, cols].astype(jnp.float32)
    for chunk in range(chunks):
        cols = slice(chunk * LANES, (chunk + 1) * LANES)

        def step(index, carry):
            low = pl.multiple_of(index * block, block)
            acc = x_ref[chunk, pl.ds(low + HALO, block), :]
            for tap in range(KERNEL):
                acc = acc + w_ref[chunk, tap : tap + 1, :] * x_ref[
                    chunk, pl.ds(low + HALO + HALF - tap, block), :
                ]
            out_ref[pl.ds(low, block), cols] = acc.astype(jnp.bfloat16)
            return carry

        lax.fori_loop(0, frames // block, step, 0)


def tile_of(frames):
    for tile in (256, 128, 64, 32, 16):
        if frames % tile == 0:
            return tile
    return frames


def params(mib=None):
    return pltpu.CompilerParams(vmem_limit_bytes=None if mib is None else mib << 20)


def relayed(tokens, width):
    groups = lax.axis_size("tm") % 4 == 0
    return groups and lax.axis_size("mp") == 2 and width % 384 == 0 and tokens % LANES == 0


def attention(queries, upstream, bounds, frame_keys, frame_values):
    frames, width = frame_keys.shape
    tokens = queries.shape[0]
    heads = width // HD
    window = window_of(width)
    scale = 1.0 / math.sqrt(HD)
    tile = tile_of(frames)
    f32, bf16 = jnp.float32, jnp.bfloat16
    keys_t = frame_keys.T
    shape = jax.ShapeDtypeStruct
    masks = [
        pltpu.VMEM((heads, tokens, window), bf16),
        pltpu.VMEM((heads, tokens, window), bf16),
        pltpu.VMEM((frames, tokens), f32),
    ]
    stat = shape((3 * heads, tokens), f32)
    work = 2 * tokens * frames * width
    peers = lax.axis_size("tm")

    def grads(offsets, guests):
        n_stats = tuple(len(guest) - 3 for guest in guests)
        arrays = [x for guest in guests for x in guest]
        return pl.pallas_call(
            functools.partial(grads_kernel, offsets, n_stats, tile, scale),
            out_shape=[shape((frames, width), bf16)] * 2
            + [shape((tokens, width), bf16)] * 2
            + [shape((tokens, width), f32)],
            in_specs=[VMEM] * (3 + len(arrays)),
            out_specs=[VMEM] * 5,
            scratch_shapes=masks
            + [pltpu.VMEM((2 * heads, tokens), f32), pltpu.VMEM((width, tokens), f32)]
            + [pltpu.VMEM((frames, width), f32)] * 2,
            compiler_params=params(40),
            cost_estimate=pl.CostEstimate(
                flops=30 * work, bytes_accessed=20 * frames * width, transcendentals=0
            ),
            name="grads",
        )(frame_keys, frame_values, keys_t, *arrays)

    if relayed(tokens, width):
        wide = shape((2, tokens, width), bf16)
        steps = 2 * (width // LANES)
        dma = pltpu.SemaphoreType.DMA
        near, far, rel, own_stats, here, peer, back = pl.pallas_call(
            functools.partial(exchange_kernel, tile, scale),
            out_shape=[wide, wide, shape((3, 2, tokens), jnp.int32), stat]
            + [shape((2, 3 * heads, tokens), f32)] * 3,
            in_specs=[VMEM] * 5,
            out_specs=[VMEM] * 7,
            scratch_shapes=[
                pltpu.VMEM((2, tokens, width), bf16),
                pltpu.VMEM((2, tokens), jnp.int32),
                pltpu.VMEM((2, tokens), jnp.int32),
                pltpu.VMEM((3, frames, tokens), f32),
                pltpu.VMEM((2, tokens, window), bf16),
                pltpu.VMEM((2, tokens, window), bf16),
                dma((3, steps)), dma((steps,)), dma((steps,)), dma((steps,)),
                dma((4,)), dma((4,)), dma((2,)), dma((2,)),
            ],
            compiler_params=pltpu.CompilerParams(
                collective_id=0, has_side_effects=True, vmem_limit_bytes=32 << 20
            ),
            name="exchange",
        )(queries, upstream, bounds.T, frame_keys, frame_values)
        key_low, value_low, near_dq, far_dq, own_dq = grads(
            (0, 0, 0),
            (
                (near[0], near[1], rel[1], here[0], peer[0]),
                (far[0], far[1], rel[2], here[1], peer[1]),
                (queries, upstream, rel[0], own_stats, back[0], back[1]),
            ),
        )
        terms = (
            lax.ppermute(near_dq, "tm", [(i, i ^ 1) for i in range(peers)]),
            lax.ppermute(
                far_dq,
                "tm",
                [(i, i - 1 + 2 * (i % 2)) for i in range(peers) if 0 <= i - 1 + 2 * (i % 2) < peers],
            ),
        )
    else:
        base = lax.axis_index("tm") * frames
        own = (queries, upstream, (bounds - base).T)
        prev = tuple(shifted(x, "tm", 1) for x in own)
        after = tuple(shifted(x, "tm", -1) for x in own)

        def stats(offsets, guests):
            return pl.pallas_call(
                functools.partial(stats_kernel, offsets, tile, scale),
                out_shape=[stat] * len(offsets),
                in_specs=[VMEM] * (2 + 3 * len(offsets)),
                out_specs=[VMEM] * len(offsets),
                scratch_shapes=masks,
                compiler_params=params(24),
                name="stats%d" % len(offsets),
            )(frame_keys, frame_values, *[x for guest in guests for x in guest])

        (own_stats,) = stats((0,), (own,))
        prev_own = shifted(own_stats, "tm", 1)
        after_own = shifted(own_stats, "tm", -1)
        prev_stats, after_stats = stats((-frames, frames), (prev, after))
        from_after = shifted(prev_stats, "tm", -1)
        from_prev = shifted(after_stats, "tm", 1)
        position = lax.axis_index("tm")
        empty = jnp.where(jnp.arange(3 * heads) < heads, masked_fill, 0.0).astype(f32)[:, None]
        from_prev = jnp.where(position == 0, empty, from_prev)
        from_after = jnp.where(position == peers - 1, empty, from_after)
        key_low, value_low, prev_dq, after_dq, own_dq = grads(
            (-frames, frames, 0),
            (
                (*prev, prev_stats, prev_own),
                (*after, after_stats, after_own),
                (*own, own_stats, from_prev, from_after),
            ),
        )
        terms = (shifted(prev_dq, "tm", -1), shifted(after_dq, "tm", 1))
    query_gradient = own_dq + terms[0].astype(f32) + terms[1].astype(f32)
    return key_low, value_low, query_gradient.astype(bf16)


def depthwise(hidden_gradient, kernel_taps):
    frames, width = hidden_gradient.shape
    before = shifted(hidden_gradient[frames - HALO :], "tm", 1)
    after = shifted(hidden_gradient[:HALO], "tm", -1)
    chunks = width // LANES
    return pl.pallas_call(
        functools.partial(conv_kernel, tile_of(frames) // 4),
        out_shape=jax.ShapeDtypeStruct((frames, width), jnp.bfloat16),
        in_specs=[VMEM] * 4,
        out_specs=VMEM,
        scratch_shapes=[
            pltpu.VMEM((chunks, frames + 2 * HALO, LANES), jnp.float32),
            pltpu.VMEM((chunks, KERNEL + 1, LANES), jnp.float32),
        ],
        compiler_params=params(16),
        name="conv",
    )(hidden_gradient, before, after, kernel_taps)


def plain_depthwise(hidden_gradient, kernel_taps):
    frames = hidden_gradient.shape[0]
    before = shifted(hidden_gradient[frames - HALF :], "tm", 1)
    after = shifted(hidden_gradient[:HALF], "tm", -1)
    padded = jnp.concatenate([before, hidden_gradient, after], 0).astype(jnp.float32)
    weights = kernel_taps.astype(jnp.float32)
    result = hidden_gradient.astype(jnp.float32)
    for tap in range(KERNEL):
        lower = 2 * HALF - tap
        result = result + weights[tap] * padded[lower : lower + frames]
    return result.astype(jnp.bfloat16)


def mp_sum(part):
    if lax.axis_size("mp") == 2:
        other = lax.ppermute(part, "mp", [(0, 1), (1, 0)])
        return part.astype(jnp.float32) + other.astype(jnp.float32)
    return lax.psum(part, "mp").astype(jnp.float32)


def mp_scatter(part, width):
    me = lax.axis_index("mp")
    if lax.axis_size("mp") == 2:
        mine = lax.dynamic_slice_in_dim(part, me * width, width, 1)
        theirs = lax.dynamic_slice_in_dim(part, (1 - me) * width, width, 1)
        other = lax.ppermute(theirs, "mp", [(0, 1), (1, 0)])
        return mine.astype(jnp.float32) + other.astype(jnp.float32)
    return lax.psum_scatter(part, "mp", scatter_dimension=1, tiled=True).astype(jnp.float32)


def feed_forward(key_low, value_low, hidden_pre, expand_weight, shrink_weight, key_weight, value_weight):
    frames, width = key_low.shape
    pieces = 2 if frames % 32 == 0 else 1
    size = frames // pieces
    me = lax.axis_index("mp")
    sums = []
    for piece in range(pieces):
        rows = slice(piece * size, (piece + 1) * size)
        part = contract_last(key_low[rows], key_weight) + contract_last(value_low[rows], value_weight)
        sums.append(mp_sum(part.astype(jnp.bfloat16)))
    out = []
    for piece in range(pieces):
        rows = slice(piece * size, (piece + 1) * size)
        act = 0.5 * contract_last(sums[piece].astype(jnp.bfloat16), shrink_weight)
        pre = (act * silu_slope(hidden_pre[rows].astype(jnp.float32))).astype(jnp.bfloat16)
        back = mp_scatter(contract_last(pre, expand_weight).astype(jnp.bfloat16), width)
        mine = lax.dynamic_slice_in_dim(sums[piece], me * width, width, 1)
        out.append((mine + back).astype(jnp.bfloat16))
    return jnp.concatenate(out, 0) if pieces > 1 else out[0]


def shards(
    queries,
    upstream,
    bounds,
    frame_keys,
    frame_values,
    hidden_pre,
    expand_weight,
    shrink_weight,
    key_weight,
    value_weight,
    kernel_taps,
):
    key_low, value_low, query_gradient = attention(
        queries, upstream, bounds, frame_keys, frame_values
    )
    hidden_gradient = feed_forward(
        key_low, value_low, hidden_pre, expand_weight, shrink_weight, key_weight, value_weight
    )
    if hidden_gradient.shape[1] % LANES == 0:
        frame_gradient = depthwise(hidden_gradient, kernel_taps)
    else:
        frame_gradient = plain_depthwise(hidden_gradient, kernel_taps)
    return (frame_gradient, query_gradient)


def solution(mesh):
    placed = (
        P("tm", "mp"),
        P("tm", "mp"),
        P("tm", None),
        P("tm", "mp"),
        P("tm", "mp"),
        P("tm", "mp"),
        P(None, "mp"),
        P("mp", None),
        P(None, "mp"),
        P(None, "mp"),
        P(None, "mp"),
    )
    return jax.shard_map(
        shards,
        mesh=mesh,
        in_specs=placed,
        out_specs=(P("tm", "mp"), P("tm", "mp")),
        check_vma=False,
    )
```

```python
import functools
import math

import jax
import jax.numpy as jnp
from jax import lax
from jax.experimental import pallas as pl
from jax.experimental.pallas import tpu as pltpu
from jax.sharding import PartitionSpec as P

HD = 96
KERNEL = 31
HALF = 15
LANES = 128
HALO = 16
masked_fill = -1e30
VMEM = pl.BlockSpec(memory_space=pltpu.VMEM)


def shifted(value, axis, by):
    peers = lax.axis_size(axis)
    pairs = [(i, i + by) for i in range(peers) if 0 <= i + by < peers]
    return lax.ppermute(value, axis, pairs)


def contract_last(left, right):
    return lax.dot_general(
        left, right, (((1,), (1,)), ((), ())), preferred_element_type=jnp.float32
    )


def mm(left, right):
    return jnp.dot(left, right, preferred_element_type=jnp.float32)


def silu_slope(hidden_pre):
    logistic = jax.nn.sigmoid(hidden_pre)
    return logistic * (1.0 + hidden_pre * (1.0 - logistic))


def window_of(width):
    return min(2 * LANES, width)


def window_start(pair):
    return 384 * (pair // 2) + LANES * (pair % 2)


def mask_heads(src_ref, dst_ref):
    heads, _, window = dst_ref.shape
    column = lax.broadcasted_iota(jnp.int32, (1, window), 1)
    for head in range(heads):
        low = window_start(head // 2)
        at = head * HD - low
        keep = jnp.where((column >= at) & (column < at + HD), 1.0, 0.0).astype(jnp.bfloat16)
        dst_ref[head] = src_ref[:, low : low + window] * keep


def frame_tiles(bounds_ref, bias_ref, offset, tile, body):
    frames, tokens = bias_ref.shape
    begin = bounds_ref[0:1, :] + offset
    end = bounds_ref[1:2, :] + offset
    for index in range(frames // tile):
        low = index * tile
        touch = (begin < low + tile) & (end > low)
        active = jnp.max(jnp.where(touch, 1.0, 0.0)) > 0.0

        @pl.when(active)
        def _():
            row = low + lax.broadcasted_iota(jnp.int32, (tile, tokens), 0)
            inside = (row >= begin) & (row < end)
            bias_ref[low : low + tile, :] = jnp.where(inside, 0.0, masked_fill)
            body(low)


def stats_kernel(offsets, tile, scale, k_ref, v_ref, *refs):
    guests = len(offsets)
    inputs, outputs = refs[: 3 * guests], refs[3 * guests : 4 * guests]
    qm_ref, um_ref, bias_ref = refs[4 * guests :]
    heads, tokens, window = qm_ref.shape
    for guest, offset in enumerate(offsets):
        q_ref, u_ref, b_ref = inputs[3 * guest : 3 * guest + 3]
        out = outputs[guest]
        mask_heads(q_ref, qm_ref)
        mask_heads(u_ref, um_ref)
        out[0:heads, :] = jnp.full((heads, tokens), masked_fill, jnp.float32)
        out[heads:, :] = jnp.zeros((2 * heads, tokens), jnp.float32)

        def body(low):
            def pair_step(pair, carry):
                cols = pl.ds(pl.multiple_of(window_start(pair), LANES), window)
                keys = k_ref[low : low + tile, cols]
                values = v_ref[low : low + tile, cols]
                bias = bias_ref[low : low + tile, :]
                for side in range(2):
                    head = 2 * pair + side
                    scores = contract_last(keys, qm_ref[head]) + bias
                    slopes = contract_last(values, um_ref[head])
                    old = out[pl.ds(head, 1), :]
                    new = jnp.maximum(old, jnp.max(scores, 0, keepdims=True))
                    fade = jnp.exp((old - new) * scale)
                    expos = jnp.exp((scores - new) * scale)
                    out[pl.ds(head, 1), :] = new
                    out[pl.ds(heads + head, 1), :] = out[
                        pl.ds(heads + head, 1), :
                    ] * fade + jnp.sum(expos, 0, keepdims=True)
                    out[pl.ds(2 * heads + head, 1), :] = out[
                        pl.ds(2 * heads + head, 1), :
                    ] * fade + jnp.sum(expos * slopes, 0, keepdims=True)
                return carry

            lax.fori_loop(0, heads // 2, pair_step, 0)

        frame_tiles(b_ref, bias_ref, offset, tile, body)


def bias_from(bounds_ref, bias_ref, tile):
    frames, tokens = bias_ref.shape
    begin, end = bounds_ref[0:1, :], bounds_ref[1:2, :]

    def step(index, carry):
        low = pl.multiple_of(index * tile, tile)
        row = low + lax.broadcasted_iota(jnp.int32, (tile, tokens), 0)
        inside = (row >= begin) & (row < end)
        bias_ref[pl.ds(low, tile), :] = jnp.where(inside, 0.0, masked_fill)
        return carry

    lax.fori_loop(0, frames // tile, step, 0)


def pair_stats(pair, tile, scale, k_ref, v_ref, q, u, bias_ref, out, qm_ref, um_ref):
    frames, tokens = bias_ref.shape
    _, _, window = qm_ref.shape
    heads = out.shape[0] // 3
    low = window_start(pair)
    cols = slice(low, low + window)
    column = lax.broadcasted_iota(jnp.int32, (1, window), 1)
    for side in range(2):
        at = (2 * pair + side) * HD - low
        keep = jnp.where((column >= at) & (column < at + HD), 1.0, 0.0).astype(jnp.bfloat16)
        qm_ref[side] = q[:, cols] * keep
        um_ref[side] = u[:, cols] * keep

    def step(index, carry):
        rows = pl.ds(pl.multiple_of(index * tile, tile), tile)
        keys, values = k_ref[rows, cols], v_ref[rows, cols]
        bias = bias_ref[rows, :]
        result = []
        for side in range(2):
            old, total, weighted = carry[3 * side : 3 * side + 3]
            scores = contract_last(keys, qm_ref[side]) + bias
            slopes = contract_last(values, um_ref[side])
            new = jnp.maximum(old, jnp.max(scores, 0, keepdims=True))
            fade = jnp.exp((old - new) * scale)
            expos = jnp.exp((scores - new) * scale)
            result += [
                new,
                total * fade + jnp.sum(expos, 0, keepdims=True),
                weighted * fade + jnp.sum(expos * slopes, 0, keepdims=True),
            ]
        return tuple(result)

    zero = jnp.zeros((1, tokens), jnp.float32)
    start = (zero + masked_fill, zero, zero)
    done = lax.fori_loop(0, frames // tile, step, start + start)
    for side in range(2):
        head = 2 * pair + side
        for kind in range(3):
            out[kind * heads + head : kind * heads + head + 1, :] = done[3 * side + kind]


def exchange_kernel(
    tile, scale, q_ref, u_ref, b_ref, k_ref, v_ref,
    near, far, rel, own_ref, here_ref, peer_ref, back_ref,
    transit, b_near, b_far, bias_ref, qm_ref, um_ref, send, recv_near, recv_y, recv_far,
    stat_send, stat_recv, b_send, b_recv,
):
    me = lax.axis_index("tm")
    count = lax.axis_size("tm")
    frames = k_ref.shape[0]
    heads = own_ref.shape[0] // 3
    place = lax.rem(me, 4)
    odd = lax.rem(me, 2)
    x_peer = me + 1 - 2 * odd
    y_peer = jnp.where(place < 2, me + 2, me - 2)
    far_peer = me - 1 + 2 * odd
    has_far = (far_peer >= 0) & (far_peer < count)
    corner = (place == 0) | (place == 3)
    up = jnp.where(place == 0, me + 4, me - 4)
    down = jnp.where(place == 0, me - 4, me + 4)
    has_up = corner & (up >= 0) & (up < count)
    has_down = corner & (down >= 0) & (down < count)

    barrier = pltpu.get_barrier_semaphore()

    def greet(peer):
        pl.semaphore_signal(
            barrier, inc=1, device_id={"tm": peer}, device_id_type=pl.DeviceIdType.MESH
        )

    greet(x_peer)
    greet(y_peer)
    pl.when(has_far)(lambda: greet(far_peer))
    pl.when(has_up)(lambda: greet(up))
    pl.when(has_down)(lambda: greet(down))
    callers = 2
    for there in (has_far, has_up, has_down):
        callers = callers + jnp.where(there, 1, 0)
    pl.semaphore_wait(barrier, callers)

    def remote(src, dst, send_sem, recv_sem, peer):
        return pltpu.make_async_remote_copy(
            src_ref=src, dst_ref=dst, send_sem=send_sem, recv_sem=recv_sem,
            device_id={"tm": peer}, device_id_type=pl.DeviceIdType.MESH,
        )

    steps = 2 * (q_ref.shape[1] // LANES)

    def part(c):
        return slice((c // 2) * LANES, (c // 2 + 1) * LANES)

    def first(c):
        src = q_ref if c % 2 == 0 else u_ref
        return remote(
            src.at[:, part(c)], near.at[c % 2, :, part(c)], send.at[0, c], recv_near.at[c], x_peer
        )

    def second_final(c):
        return remote(
            near.at[c % 2, :, part(c)], far.at[c % 2, :, part(c)], send.at[1, c], recv_far.at[c], y_peer
        )

    def second_transit(c):
        return remote(
            near.at[c % 2, :, part(c)], transit.at[c % 2, :, part(c)], send.at[1, c], recv_y.at[c], y_peer
        )

    def third(c):
        return remote(
            transit.at[c % 2, :, part(c)], far.at[c % 2, :, part(c)], send.at[2, c], recv_far.at[c], up
        )

    to_near = remote(b_ref, b_near, b_send.at[0], b_recv.at[0], x_peer)
    to_far = remote(b_ref, b_far, b_send.at[1], b_recv.at[1], far_peer)
    to_near.start()
    pl.when(has_far)(lambda: to_far.start())
    for c in range(steps):
        first(c).start()

    @pl.when(jnp.logical_not(has_far))
    def _():
        far[...] = jnp.zeros_like(far)
        b_far[...] = jnp.zeros_like(b_far)
        peer_ref[1] = jnp.zeros_like(own_ref)
        back_ref[1, 0:heads, :] = jnp.full((heads, own_ref.shape[1]), masked_fill, jnp.float32)
        back_ref[1, heads:, :] = jnp.zeros((2 * heads, own_ref.shape[1]), jnp.float32)

    base = me * frames
    rel[0] = b_ref[...] - base
    bias_from(rel.at[0], bias_ref.at[0], tile)

    own_sends = [
        remote(own_ref, peer_ref.at[0], stat_send.at[0], stat_recv.at[0], x_peer),
        remote(own_ref, peer_ref.at[1], stat_send.at[1], stat_recv.at[1], far_peer),
    ]
    back_sends = [
        remote(here_ref.at[0], back_ref.at[0], stat_send.at[2], stat_recv.at[2], x_peer),
        remote(here_ref.at[1], back_ref.at[1], stat_send.at[3], stat_recv.at[3], far_peer),
    ]

    def own_unit(pair):
        pair_stats(pair, tile, scale, k_ref, v_ref, q_ref, u_ref, bias_ref.at[0], own_ref, qm_ref, um_ref)
        if pair == heads // 2 - 1:
            own_sends[0].start()
            pl.when(has_far)(lambda: own_sends[1].start())

    def near_unit(pair):
        pair_stats(
            pair, tile, scale, k_ref, v_ref, near.at[0], near.at[1], bias_ref.at[1], here_ref.at[0], qm_ref, um_ref
        )
        if pair == heads // 2 - 1:
            back_sends[0].start()

    def far_unit(pair):
        pair_stats(
            pair, tile, scale, k_ref, v_ref, far.at[0], far.at[1], bias_ref.at[2], here_ref.at[1], qm_ref, um_ref
        )

    def need(pair):
        return 2 * ((window_start(pair) + 2 * LANES) // LANES)

    waited_far = [0]
    passed_y = [0]

    def pass_on(upto):
        while passed_y[0] < upto:
            c = passed_y[0]

            @pl.when(corner)
            def _():
                second_transit(c).wait_recv()
                pl.when(has_up)(lambda: third(c).start())

            passed_y[0] += 1

    def far_ready(upto):
        while waited_far[0] < upto:
            c = waited_far[0]
            pl.when(has_far)(lambda: second_final(c).wait_recv())
            waited_far[0] += 1

    pairs = heads // 2
    near_next, own_next, far_next = 0, 0, 0
    for c in range(steps):
        first(c).wait_recv()
        pl.when(corner)(lambda: second_final(c).start())
        pl.when(jnp.logical_not(corner))(lambda: second_transit(c).start())
        pass_on(c - 1)
        if c == 0:
            to_near.wait_recv()
            rel[1] = b_near[...] - base
            bias_from(rel.at[1], bias_ref.at[1], tile)
        if own_next < pairs:
            own_unit(own_next)
            own_next += 1
        elif near_next < pairs and need(near_next) <= c + 1:
            near_unit(near_next)
            near_next += 1
        elif far_next < pairs and need(far_next) <= c - 3:
            if far_next == 0:
                pl.when(has_far)(lambda: to_far.wait_recv())
                rel[2] = b_far[...] - base
                bias_from(rel.at[2], bias_ref.at[2], tile)
            far_ready(need(far_next))
            far_unit(far_next)
            far_next += 1
    while passed_y[0] < steps or near_next < pairs or far_next < pairs:
        pass_on(min(steps, passed_y[0] + 1 if passed_y[0] < steps - 2 else steps))
        if near_next < pairs:
            near_unit(near_next)
            near_next += 1
            continue
        if far_next < pairs:
            if far_next == 0:
                pl.when(has_far)(lambda: to_far.wait_recv())
                rel[2] = b_far[...] - base
                bias_from(rel.at[2], bias_ref.at[2], tile)
            if need(far_next) > steps - 4:
                pass_on(steps)
            far_ready(need(far_next))
            far_unit(far_next)
            far_next += 1
    far_ready(steps)
    pl.when(has_far)(lambda: back_sends[1].start())

    to_near.wait_send()
    pl.when(has_far)(lambda: to_far.wait_send())
    for c in range(steps):
        first(c).wait_send()
        second_final(c).wait_send()
        pl.when(has_up)(lambda: third(c).wait_send())
    own_sends[0].wait()
    back_sends[0].wait()

    @pl.when(has_far)
    def _():
        own_sends[1].wait()
        back_sends[1].wait()


def grads_kernel(offsets, n_stats, tile, scale, k_ref, v_ref, kt_ref, *refs):
    guests = len(offsets)
    inputs = []
    for kinds in n_stats:
        inputs.append(refs[: 3 + kinds])
        refs = refs[3 + kinds :]
    dk_out, dv_out = refs[:2]
    dq_outs = refs[2 : 2 + guests]
    qm_ref, um_ref, bias_ref, norm_ref, dqt_ref, dk_ref, dv_ref = refs[2 + guests :]
    dk_ref[...] = jnp.zeros_like(dk_ref)
    dv_ref[...] = jnp.zeros_like(dv_ref)
    heads, tokens, window = qm_ref.shape
    for guest, offset in enumerate(offsets):
        q_ref, u_ref, b_ref = inputs[guest][:3]
        stats = [r[...] for r in inputs[guest][3:]]
        peak = stats[0][0:heads]
        for one in stats[1:]:
            peak = jnp.maximum(peak, one[0:heads])
        total = jnp.zeros_like(peak)
        weighted = jnp.zeros_like(peak)
        for one in stats:
            factor = jnp.exp((one[0:heads] - peak) * scale)
            total = total + one[heads : 2 * heads] * factor
            weighted = weighted + one[2 * heads :] * factor
        total = jnp.where(total > 0.0, total, 1.0)
        norm_ref[0:heads, :] = peak * scale + jnp.log(total)
        norm_ref[heads:, :] = weighted / total
        mask_heads(q_ref, qm_ref)
        mask_heads(u_ref, um_ref)
        dqt_ref[...] = jnp.zeros_like(dqt_ref)

        def body(low):
            def pair_step(pair, carry):
                cols = pl.ds(pl.multiple_of(window_start(pair), LANES), window)
                keys = k_ref[low : low + tile, cols]
                values = v_ref[low : low + tile, cols]
                inside = bias_ref[low : low + tile, :] == 0.0
                key_term = value_term = None
                for side in range(2):
                    head = 2 * pair + side
                    scores = contract_last(keys, qm_ref[head])
                    slopes = contract_last(values, um_ref[head])
                    log_total = norm_ref[pl.ds(head, 1), :]
                    delta = norm_ref[pl.ds(heads + head, 1), :]
                    probs = jnp.where(inside, jnp.exp(scores * scale - log_total), 0.0)
                    grad = (probs * ((slopes - delta) * scale)).astype(jnp.bfloat16)
                    key_one = mm(grad, qm_ref[head])
                    value_one = mm(probs.astype(jnp.bfloat16), um_ref[head])
                    key_term = key_one if side == 0 else key_term + key_one
                    value_term = value_one if side == 0 else value_term + value_one
                    rows = pl.ds(pl.multiple_of(head * HD, HD // 3), HD)
                    dqt_ref[rows, :] += mm(kt_ref[rows, low : low + tile], grad)
                dk_ref[low : low + tile, cols] += key_term
                dv_ref[low : low + tile, cols] += value_term
                return carry

            lax.fori_loop(0, heads // 2, pair_step, 0)

        frame_tiles(b_ref, bias_ref, offset, tile, body)
        dq_outs[guest][...] = dqt_ref[...].T.astype(dq_outs[guest].dtype)
    dk_out[...] = dk_ref[...].astype(jnp.bfloat16)
    dv_out[...] = dv_ref[...].astype(jnp.bfloat16)


def conv_kernel(block, h_ref, before_ref, after_ref, taps_ref, out_ref, x_ref, w_ref):
    chunks, rows, _ = x_ref.shape
    frames = rows - 2 * HALO
    for chunk in range(chunks):
        cols = slice(chunk * LANES, (chunk + 1) * LANES)
        x_ref[chunk, 0:HALO, :] = before_ref[:, cols].astype(jnp.float32)
        x_ref[chunk, HALO : HALO + frames, :] = h_ref[:, cols].astype(jnp.float32)
        x_ref[chunk, HALO + frames :, :] = after_ref[:, cols].astype(jnp.float32)
        w_ref[chunk, 0:KERNEL, :] = taps_ref[:, cols].astype(jnp.float32)
    for chunk in range(chunks):
        cols = slice(chunk * LANES, (chunk + 1) * LANES)

        def step(index, carry):
            low = pl.multiple_of(index * block, block)
            acc = x_ref[chunk, pl.ds(low + HALO, block), :]
            for tap in range(KERNEL):
                acc = acc + w_ref[chunk, tap : tap + 1, :] * x_ref[
                    chunk, pl.ds(low + HALO + HALF - tap, block), :
                ]
            out_ref[pl.ds(low, block), cols] = acc.astype(jnp.bfloat16)
            return carry

        lax.fori_loop(0, frames // block, step, 0)


def tail_kernel(
    rows, block, kl_ref, vl_ref, near_dq, far_dq, own_dq, taps_ref,
    hidden_hbm, ew_hbm, sw_hbm, kw_hbm, vw_hbm,
    out_ref, query_ref,
    hidden_ref, ew_ref, sw_ref, kw_ref, vw_ref,
    part, part_in, pre, theirs, theirs_in, mine, low_ref, edge, edge_in, terms,
    x_ref, w_ref, load, send, recv, send_part, recv_part, send_back, recv_back,
):
    me = lax.axis_index("tm")
    side = lax.axis_index("mp")
    count = lax.axis_size("tm")
    frames, width = kl_ref.shape
    units = sw_ref.shape[0]
    full = kw_ref.shape[0]
    step_cols = 2 * LANES
    odd = lax.rem(me, 2)
    near_peer = me + 1 - 2 * odd
    far_peer = me - 1 + 2 * odd
    has_far = (far_peer >= 0) & (far_peer < count)
    other = 1 - side

    loads = [
        pltpu.make_async_copy(src, dst, load.at[i])
        for i, (src, dst) in enumerate(
            ((kw_hbm, kw_ref), (vw_hbm, vw_ref), (sw_hbm, sw_ref), (hidden_hbm, hidden_ref), (ew_hbm, ew_ref))
        )
    ]
    for one in loads:
        one.start()

    barrier = pltpu.get_barrier_semaphore()
    mesh = pl.DeviceIdType.MESH
    pl.semaphore_signal(barrier, inc=1, device_id={"mp": other}, device_id_type=mesh)
    pl.semaphore_signal(barrier, inc=1, device_id={"tm": near_peer}, device_id_type=mesh)

    @pl.when(has_far)
    def _():
        pl.semaphore_signal(barrier, inc=1, device_id={"tm": far_peer}, device_id_type=mesh)

    def remote(src, dst, send_sem, recv_sem, peer):
        return pltpu.make_async_remote_copy(
            src_ref=src, dst_ref=dst, send_sem=send_sem, recv_sem=recv_sem,
            device_id=peer, device_id_type=mesh,
        )

    near, far, twin = {"tm": near_peer}, {"tm": far_peer}, {"mp": other}
    query_sends = (
        remote(near_dq, terms.at[0], send.at[0], recv.at[0], near),
        remote(far_dq, terms.at[1], send.at[1], recv.at[1], far),
    )
    near_row = pl.multiple_of(jnp.where(odd == 1, 0, frames - HALO), HALO)
    far_row = pl.multiple_of(jnp.where(odd == 1, frames - HALO, 0), HALO)
    edge_sends = (
        remote(edge.at[0], edge_in.at[0], send.at[2], recv.at[2], near),
        remote(edge.at[1], edge_in.at[1], send.at[3], recv.at[3], far),
    )

    def part_send(piece):
        at = pl.ds(piece * rows, rows)
        return remote(part.at[at], part_in.at[at], send_part.at[piece], recv_part.at[piece], twin)

    def back_send(piece):
        at = pl.ds(piece * rows, rows)
        return remote(theirs.at[at], theirs_in.at[at], send_back.at[piece], recv_back.at[piece], twin)

    chunks = width // LANES
    for chunk in range(chunks):
        cols = slice(chunk * LANES, (chunk + 1) * LANES)
        w_ref[chunk, 0:KERNEL, :] = taps_ref[:, cols].astype(jnp.float32)

    pieces = frames // rows
    order = [0] + ([pieces - 1] if pieces > 1 else []) + list(range(1, pieces - 1))
    loads[0].wait()
    loads[1].wait()
    for number, piece in enumerate(order):
        at = slice(piece * rows, (piece + 1) * rows)

        def encode(index, carry):
            cols = pl.ds(pl.multiple_of(index * step_cols, step_cols), step_cols)
            total = contract_last(kl_ref[at, :], kw_ref[cols, :]) + contract_last(
                vl_ref[at, :], vw_ref[cols, :]
            )
            part[at, cols] = total.astype(jnp.bfloat16)
            return carry

        lax.fori_loop(0, full // step_cols, encode, 0)
        if number == 0:
            callers = 2 + jnp.where(has_far, 1, 0)
            pl.semaphore_wait(barrier, callers)
        part_send(piece).start()
        if number == 0:
            query_sends[0].start()
            pl.when(has_far)(lambda: query_sends[1].start())

    def feed(piece):
        at = slice(piece * rows, (piece + 1) * rows)
        part_send(piece).wait_recv()
        low_ref[...] = (
            part[at, :].astype(jnp.float32) + part_in[at, :].astype(jnp.float32)
        ).astype(jnp.bfloat16)

        def act(index, carry):
            cols = pl.ds(pl.multiple_of(index * step_cols, step_cols), step_cols)
            slope = silu_slope(hidden_ref[at, cols].astype(jnp.float32))
            gain = 0.5 * contract_last(low_ref[...], sw_ref[cols, :])
            pre[:, cols] = (gain * slope).astype(jnp.bfloat16)
            return carry

        lax.fori_loop(0, units // step_cols, act, 0)

        def back(whose, dst):
            def step(index, carry):
                first = pl.multiple_of(index * step_cols, step_cols)
                source = pl.ds(pl.multiple_of(whose * width + first, step_cols), step_cols)
                dst[at, pl.ds(first, step_cols)] = contract_last(
                    pre[...], ew_ref[source, :]
                ).astype(jnp.bfloat16)
                return carry

            lax.fori_loop(0, width // step_cols, step, 0)

        back(other, theirs)
        back_send(piece).start()
        back(side, mine)

    def finish(piece):
        at = slice(piece * rows, (piece + 1) * rows)
        back_send(piece).wait_recv()

        def step(chunk, carry):
            cols = pl.ds(pl.multiple_of(chunk * LANES, LANES), LANES)
            own = pl.ds(pl.multiple_of(side * width + chunk * LANES, LANES), LANES)
            total = part[at, own].astype(jnp.float32) + part_in[at, own].astype(jnp.float32)
            back = mine[at, cols].astype(jnp.float32) + theirs_in[at, cols].astype(jnp.float32)
            low = (total + back).astype(jnp.bfloat16)
            mine[at, cols] = low
            x_ref[chunk, HALO + piece * rows : HALO + (piece + 1) * rows, :] = low.astype(jnp.float32)
            return carry

        lax.fori_loop(0, chunks, step, 0)

    def send_edges():
        edge[0] = mine[pl.ds(near_row, HALO), :]
        edge[1] = mine[pl.ds(far_row, HALO), :]
        edge_sends[0].start()
        pl.when(has_far)(lambda: edge_sends[1].start())

    loads[2].wait()
    loads[3].wait()
    loads[4].wait()
    for number, piece in enumerate(order):
        feed(piece)
        if number >= 1:
            finish(order[number - 1])
        if number == 2:
            send_edges()
    finish(order[-1])
    if len(order) < 3:
        send_edges()

    def conv(chunk, low):
        acc = x_ref[chunk, pl.ds(low + HALO, block), :]
        for tap in range(KERNEL):
            acc = acc + w_ref[chunk, tap : tap + 1, :] * x_ref[
                chunk, pl.ds(low + HALO + HALF - tap, block), :
            ]
        cols = pl.ds(pl.multiple_of(chunk * LANES, LANES), LANES)
        out_ref[pl.ds(low, block), cols] = acc.astype(jnp.bfloat16)

    blocks = frames // block

    def inner(index, carry):
        conv(index // (blocks - 2), pl.multiple_of((1 + index % (blocks - 2)) * block, block))
        return carry

    lax.fori_loop(0, chunks * (blocks - 2), inner, 0)

    edge_sends[0].wait()

    @pl.when(has_far)
    def _():
        edge_sends[1].wait()

    @pl.when(jnp.logical_not(has_far))
    def _():
        edge_in[1] = jnp.zeros((HALO, width), jnp.bfloat16)
        terms[1] = jnp.zeros((terms.shape[1], width), jnp.bfloat16)

    near_at = pl.multiple_of(jnp.where(odd == 1, 0, frames + HALO), HALO)
    far_at = pl.multiple_of(jnp.where(odd == 1, frames + HALO, 0), HALO)
    for chunk in range(chunks):
        cols = slice(chunk * LANES, (chunk + 1) * LANES)
        x_ref[chunk, pl.ds(near_at, HALO), :] = edge_in[0, :, cols].astype(jnp.float32)
        x_ref[chunk, pl.ds(far_at, HALO), :] = edge_in[1, :, cols].astype(jnp.float32)

    def outer(index, carry):
        conv(index // 2, pl.multiple_of((index % 2) * (blocks - 1) * block, block))
        return carry

    lax.fori_loop(0, chunks * 2, outer, 0)

    query_sends[0].wait()
    pl.when(has_far)(lambda: query_sends[1].wait())
    query_ref[...] = (
        own_dq[...] + terms[0].astype(jnp.float32) + terms[1].astype(jnp.float32)
    ).astype(jnp.bfloat16)
    for piece in order:
        part_send(piece).wait_send()
        back_send(piece).wait_send()


def tail(
    key_low, value_low, near_dq, far_dq, own_dq,
    hidden_pre, expand_weight, shrink_weight, key_weight, value_weight, kernel_taps,
):
    frames, width = key_low.shape
    tokens = own_dq.shape[0]
    full, units = key_weight.shape[0], shrink_weight.shape[0]
    rows = tile_of(frames)
    pieces = frames // rows
    bf16, f32 = jnp.bfloat16, jnp.float32
    chunks = width // LANES
    dma = pltpu.SemaphoreType.DMA
    weights = (hidden_pre, expand_weight, shrink_weight, key_weight, value_weight)
    return pl.pallas_call(
        functools.partial(tail_kernel, rows, rows // 4),
        out_shape=[
            jax.ShapeDtypeStruct((frames, width), bf16),
            jax.ShapeDtypeStruct((tokens, width), bf16),
        ],
        in_specs=[VMEM] * 6 + [pl.BlockSpec(memory_space=pl.ANY)] * 5,
        out_specs=[VMEM] * 2,
        scratch_shapes=[pltpu.VMEM(w.shape, bf16) for w in weights]
        + [
            pltpu.VMEM((frames, full), bf16),
            pltpu.VMEM((frames, full), bf16),
            pltpu.VMEM((rows, units), bf16),
            pltpu.VMEM((frames, width), bf16),
            pltpu.VMEM((frames, width), bf16),
            pltpu.VMEM((frames, width), bf16),
            pltpu.VMEM((rows, full), bf16),
            pltpu.VMEM((2, HALO, width), bf16),
            pltpu.VMEM((2, HALO, width), bf16),
            pltpu.VMEM((2, tokens, width), bf16),
            pltpu.VMEM((chunks, frames + 2 * HALO, LANES), f32),
            pltpu.VMEM((chunks, KERNEL + 1, LANES), f32),
            dma((5,)), dma((4,)), dma((4,)),
            dma((pieces,)), dma((pieces,)), dma((pieces,)), dma((pieces,)),
        ],
        compiler_params=pltpu.CompilerParams(
            collective_id=1, has_side_effects=True, vmem_limit_bytes=56 << 20
        ),
        name="tail",
    )(key_low, value_low, near_dq, far_dq, own_dq, kernel_taps, *weights)


def tile_of(frames):
    for tile in (256, 128, 64, 32, 16):
        if frames % tile == 0:
            return tile
    return frames


def params(mib=None):
    return pltpu.CompilerParams(vmem_limit_bytes=None if mib is None else mib << 20)


def relayed(tokens, width):
    groups = lax.axis_size("tm") % 4 == 0
    return groups and lax.axis_size("mp") == 2 and width % 384 == 0 and tokens % LANES == 0


def attention(queries, upstream, bounds, frame_keys, frame_values):
    frames, width = frame_keys.shape
    tokens = queries.shape[0]
    heads = width // HD
    window = window_of(width)
    scale = 1.0 / math.sqrt(HD)
    tile = tile_of(frames)
    f32, bf16 = jnp.float32, jnp.bfloat16
    keys_t = frame_keys.T
    shape = jax.ShapeDtypeStruct
    masks = [
        pltpu.VMEM((heads, tokens, window), bf16),
        pltpu.VMEM((heads, tokens, window), bf16),
        pltpu.VMEM((frames, tokens), f32),
    ]
    stat = shape((3 * heads, tokens), f32)
    work = 2 * tokens * frames * width
    peers = lax.axis_size("tm")

    def grads(offsets, guests):
        n_stats = tuple(len(guest) - 3 for guest in guests)
        arrays = [x for guest in guests for x in guest]
        return pl.pallas_call(
            functools.partial(grads_kernel, offsets, n_stats, tile, scale),
            out_shape=[shape((frames, width), bf16)] * 2
            + [shape((tokens, width), bf16)] * 2
            + [shape((tokens, width), f32)],
            in_specs=[VMEM] * (3 + len(arrays)),
            out_specs=[VMEM] * 5,
            scratch_shapes=masks
            + [pltpu.VMEM((2 * heads, tokens), f32), pltpu.VMEM((width, tokens), f32)]
            + [pltpu.VMEM((frames, width), f32)] * 2,
            compiler_params=params(40),
            cost_estimate=pl.CostEstimate(
                flops=30 * work, bytes_accessed=20 * frames * width, transcendentals=0
            ),
            name="grads",
        )(frame_keys, frame_values, keys_t, *arrays)

    if relayed(tokens, width):
        wide = shape((2, tokens, width), bf16)
        steps = 2 * (width // LANES)
        dma = pltpu.SemaphoreType.DMA
        near, far, rel, own_stats, here, peer, back = pl.pallas_call(
            functools.partial(exchange_kernel, tile, scale),
            out_shape=[wide, wide, shape((3, 2, tokens), jnp.int32), stat]
            + [shape((2, 3 * heads, tokens), f32)] * 3,
            in_specs=[VMEM] * 5,
            out_specs=[VMEM] * 7,
            scratch_shapes=[
                pltpu.VMEM((2, tokens, width), bf16),
                pltpu.VMEM((2, tokens), jnp.int32),
                pltpu.VMEM((2, tokens), jnp.int32),
                pltpu.VMEM((3, frames, tokens), f32),
                pltpu.VMEM((2, tokens, window), bf16),
                pltpu.VMEM((2, tokens, window), bf16),
                dma((3, steps)), dma((steps,)), dma((steps,)), dma((steps,)),
                dma((4,)), dma((4,)), dma((2,)), dma((2,)),
            ],
            compiler_params=pltpu.CompilerParams(
                collective_id=0, has_side_effects=True, vmem_limit_bytes=32 << 20
            ),
            name="exchange",
        )(queries, upstream, bounds.T, frame_keys, frame_values)
        key_low, value_low, near_dq, far_dq, own_dq = grads(
            (0, 0, 0),
            (
                (near[0], near[1], rel[1], here[0], peer[0]),
                (far[0], far[1], rel[2], here[1], peer[1]),
                (queries, upstream, rel[0], own_stats, back[0], back[1]),
            ),
        )
        return key_low, value_low, near_dq, far_dq, own_dq
    else:
        base = lax.axis_index("tm") * frames
        own = (queries, upstream, (bounds - base).T)
        prev = tuple(shifted(x, "tm", 1) for x in own)
        after = tuple(shifted(x, "tm", -1) for x in own)

        def stats(offsets, guests):
            return pl.pallas_call(
                functools.partial(stats_kernel, offsets, tile, scale),
                out_shape=[stat] * len(offsets),
                in_specs=[VMEM] * (2 + 3 * len(offsets)),
                out_specs=[VMEM] * len(offsets),
                scratch_shapes=masks,
                compiler_params=params(24),
                name="stats%d" % len(offsets),
            )(frame_keys, frame_values, *[x for guest in guests for x in guest])

        (own_stats,) = stats((0,), (own,))
        prev_own = shifted(own_stats, "tm", 1)
        after_own = shifted(own_stats, "tm", -1)
        prev_stats, after_stats = stats((-frames, frames), (prev, after))
        from_after = shifted(prev_stats, "tm", -1)
        from_prev = shifted(after_stats, "tm", 1)
        position = lax.axis_index("tm")
        empty = jnp.where(jnp.arange(3 * heads) < heads, masked_fill, 0.0).astype(f32)[:, None]
        from_prev = jnp.where(position == 0, empty, from_prev)
        from_after = jnp.where(position == peers - 1, empty, from_after)
        key_low, value_low, prev_dq, after_dq, own_dq = grads(
            (-frames, frames, 0),
            (
                (*prev, prev_stats, prev_own),
                (*after, after_stats, after_own),
                (*own, own_stats, from_prev, from_after),
            ),
        )
        terms = (shifted(prev_dq, "tm", -1), shifted(after_dq, "tm", 1))
    query_gradient = own_dq + terms[0].astype(f32) + terms[1].astype(f32)
    return key_low, value_low, query_gradient.astype(bf16)


def depthwise(hidden_gradient, kernel_taps):
    frames, width = hidden_gradient.shape
    before = shifted(hidden_gradient[frames - HALO :], "tm", 1)
    after = shifted(hidden_gradient[:HALO], "tm", -1)
    chunks = width // LANES
    return pl.pallas_call(
        functools.partial(conv_kernel, tile_of(frames) // 4),
        out_shape=jax.ShapeDtypeStruct((frames, width), jnp.bfloat16),
        in_specs=[VMEM] * 4,
        out_specs=VMEM,
        scratch_shapes=[
            pltpu.VMEM((chunks, frames + 2 * HALO, LANES), jnp.float32),
            pltpu.VMEM((chunks, KERNEL + 1, LANES), jnp.float32),
        ],
        compiler_params=params(16),
        name="conv",
    )(hidden_gradient, before, after, kernel_taps)


def plain_depthwise(hidden_gradient, kernel_taps):
    frames = hidden_gradient.shape[0]
    before = shifted(hidden_gradient[frames - HALF :], "tm", 1)
    after = shifted(hidden_gradient[:HALF], "tm", -1)
    padded = jnp.concatenate([before, hidden_gradient, after], 0).astype(jnp.float32)
    weights = kernel_taps.astype(jnp.float32)
    result = hidden_gradient.astype(jnp.float32)
    for tap in range(KERNEL):
        lower = 2 * HALF - tap
        result = result + weights[tap] * padded[lower : lower + frames]
    return result.astype(jnp.bfloat16)


def mp_sum(part):
    if lax.axis_size("mp") == 2:
        other = lax.ppermute(part, "mp", [(0, 1), (1, 0)])
        return part.astype(jnp.float32) + other.astype(jnp.float32)
    return lax.psum(part, "mp").astype(jnp.float32)


def mp_scatter(part, width):
    me = lax.axis_index("mp")
    if lax.axis_size("mp") == 2:
        mine = lax.dynamic_slice_in_dim(part, me * width, width, 1)
        theirs = lax.dynamic_slice_in_dim(part, (1 - me) * width, width, 1)
        other = lax.ppermute(theirs, "mp", [(0, 1), (1, 0)])
        return mine.astype(jnp.float32) + other.astype(jnp.float32)
    return lax.psum_scatter(part, "mp", scatter_dimension=1, tiled=True).astype(jnp.float32)


def feed_forward(key_low, value_low, hidden_pre, expand_weight, shrink_weight, key_weight, value_weight):
    frames, width = key_low.shape
    pieces = 2 if frames % 32 == 0 else 1
    size = frames // pieces
    me = lax.axis_index("mp")
    sums = []
    for piece in range(pieces):
        rows = slice(piece * size, (piece + 1) * size)
        part = contract_last(key_low[rows], key_weight) + contract_last(value_low[rows], value_weight)
        sums.append(mp_sum(part.astype(jnp.bfloat16)))
    out = []
    for piece in range(pieces):
        rows = slice(piece * size, (piece + 1) * size)
        act = 0.5 * contract_last(sums[piece].astype(jnp.bfloat16), shrink_weight)
        pre = (act * silu_slope(hidden_pre[rows].astype(jnp.float32))).astype(jnp.bfloat16)
        back = mp_scatter(contract_last(pre, expand_weight).astype(jnp.bfloat16), width)
        mine = lax.dynamic_slice_in_dim(sums[piece], me * width, width, 1)
        out.append((mine + back).astype(jnp.bfloat16))
    return jnp.concatenate(out, 0) if pieces > 1 else out[0]


def shards(
    queries,
    upstream,
    bounds,
    frame_keys,
    frame_values,
    hidden_pre,
    expand_weight,
    shrink_weight,
    key_weight,
    value_weight,
    kernel_taps,
):
    found = attention(queries, upstream, bounds, frame_keys, frame_values)
    if relayed(queries.shape[0], queries.shape[1]):
        return tail(
            *found, hidden_pre, expand_weight, shrink_weight, key_weight, value_weight, kernel_taps
        )
    key_low, value_low, query_gradient = found
    hidden_gradient = feed_forward(
        key_low, value_low, hidden_pre, expand_weight, shrink_weight, key_weight, value_weight
    )
    if hidden_gradient.shape[1] % LANES == 0:
        frame_gradient = depthwise(hidden_gradient, kernel_taps)
    else:
        frame_gradient = plain_depthwise(hidden_gradient, kernel_taps)
    return (frame_gradient, query_gradient)


def solution(mesh):
    placed = (
        P("tm", "mp"),
        P("tm", "mp"),
        P("tm", None),
        P("tm", "mp"),
        P("tm", "mp"),
        P("tm", "mp"),
        P(None, "mp"),
        P("mp", None),
        P(None, "mp"),
        P(None, "mp"),
        P(None, "mp"),
    )
    return jax.shard_map(
        shards,
        mesh=mesh,
        in_specs=placed,
        out_specs=(P("tm", "mp"), P("tm", "mp")),
        check_vma=False,
    )
```

```python
import functools
import math

import jax
import jax.numpy as jnp
from jax import lax
from jax.experimental import pallas as pl
from jax.experimental.pallas import tpu as pltpu
from jax.sharding import PartitionSpec as P

HD = 96
KERNEL = 31
HALF = 15
LANES = 128
HALO = 16
masked_fill = -1e30
VMEM = pl.BlockSpec(memory_space=pltpu.VMEM)


def shifted(value, axis, by):
    peers = lax.axis_size(axis)
    pairs = [(i, i + by) for i in range(peers) if 0 <= i + by < peers]
    return lax.ppermute(value, axis, pairs)


def contract_last(left, right):
    return lax.dot_general(
        left, right, (((1,), (1,)), ((), ())), preferred_element_type=jnp.float32
    )


def mm(left, right):
    return jnp.dot(left, right, preferred_element_type=jnp.float32)


def silu_slope(hidden_pre):
    logistic = jax.nn.sigmoid(hidden_pre)
    return logistic * (1.0 + hidden_pre * (1.0 - logistic))


def window_of(width):
    return min(2 * LANES, width)


def window_start(pair):
    return 384 * (pair // 2) + LANES * (pair % 2)


def mask_heads(src_ref, dst_ref):
    heads, _, window = dst_ref.shape
    column = lax.broadcasted_iota(jnp.int32, (1, window), 1)
    for head in range(heads):
        low = window_start(head // 2)
        at = head * HD - low
        keep = jnp.where((column >= at) & (column < at + HD), 1.0, 0.0).astype(jnp.bfloat16)
        dst_ref[head] = src_ref[:, low : low + window] * keep


def frame_tiles(bounds_ref, bias_ref, offset, tile, body):
    frames, tokens = bias_ref.shape
    begin = bounds_ref[0:1, :] + offset
    end = bounds_ref[1:2, :] + offset
    for index in range(frames // tile):
        low = index * tile
        touch = (begin < low + tile) & (end > low)
        active = jnp.max(jnp.where(touch, 1.0, 0.0)) > 0.0

        @pl.when(active)
        def _():
            row = low + lax.broadcasted_iota(jnp.int32, (tile, tokens), 0)
            inside = (row >= begin) & (row < end)
            bias_ref[low : low + tile, :] = jnp.where(inside, 0.0, masked_fill)
            body(low)


def stats_kernel(offsets, tile, scale, k_ref, v_ref, *refs):
    guests = len(offsets)
    inputs, outputs = refs[: 3 * guests], refs[3 * guests : 4 * guests]
    qm_ref, um_ref, bias_ref = refs[4 * guests :]
    heads, tokens, window = qm_ref.shape
    for guest, offset in enumerate(offsets):
        q_ref, u_ref, b_ref = inputs[3 * guest : 3 * guest + 3]
        out = outputs[guest]
        mask_heads(q_ref, qm_ref)
        mask_heads(u_ref, um_ref)
        out[0:heads, :] = jnp.full((heads, tokens), masked_fill, jnp.float32)
        out[heads:, :] = jnp.zeros((2 * heads, tokens), jnp.float32)

        def body(low):
            def pair_step(pair, carry):
                cols = pl.ds(pl.multiple_of(window_start(pair), LANES), window)
                keys = k_ref[low : low + tile, cols]
                values = v_ref[low : low + tile, cols]
                bias = bias_ref[low : low + tile, :]
                for side in range(2):
                    head = 2 * pair + side
                    scores = contract_last(keys, qm_ref[head]) + bias
                    slopes = contract_last(values, um_ref[head])
                    old = out[pl.ds(head, 1), :]
                    new = jnp.maximum(old, jnp.max(scores, 0, keepdims=True))
                    fade = jnp.exp((old - new) * scale)
                    expos = jnp.exp((scores - new) * scale)
                    out[pl.ds(head, 1), :] = new
                    out[pl.ds(heads + head, 1), :] = out[
                        pl.ds(heads + head, 1), :
                    ] * fade + jnp.sum(expos, 0, keepdims=True)
                    out[pl.ds(2 * heads + head, 1), :] = out[
                        pl.ds(2 * heads + head, 1), :
                    ] * fade + jnp.sum(expos * slopes, 0, keepdims=True)
                return carry

            lax.fori_loop(0, heads // 2, pair_step, 0)

        frame_tiles(b_ref, bias_ref, offset, tile, body)


def bias_from(bounds_ref, bias_ref, tile):
    frames, tokens = bias_ref.shape
    begin, end = bounds_ref[0:1, :], bounds_ref[1:2, :]

    def step(index, carry):
        low = pl.multiple_of(index * tile, tile)
        row = low + lax.broadcasted_iota(jnp.int32, (tile, tokens), 0)
        inside = (row >= begin) & (row < end)
        bias_ref[pl.ds(low, tile), :] = jnp.where(inside, 0.0, masked_fill)
        return carry

    lax.fori_loop(0, frames // tile, step, 0)


def pair_stats(pair, tile, scale, k_ref, v_ref, q, u, bias_ref, out, qm_ref, um_ref):
    frames, tokens = bias_ref.shape
    _, _, window = qm_ref.shape
    heads = out.shape[0] // 3
    low = window_start(pair)
    cols = slice(low, low + window)
    column = lax.broadcasted_iota(jnp.int32, (1, window), 1)
    for side in range(2):
        at = (2 * pair + side) * HD - low
        keep = jnp.where((column >= at) & (column < at + HD), 1.0, 0.0).astype(jnp.bfloat16)
        qm_ref[side] = q[:, cols] * keep
        um_ref[side] = u[:, cols] * keep

    def step(index, carry):
        rows = pl.ds(pl.multiple_of(index * tile, tile), tile)
        keys, values = k_ref[rows, cols], v_ref[rows, cols]
        bias = bias_ref[rows, :]
        result = []
        for side in range(2):
            old, total, weighted = carry[3 * side : 3 * side + 3]
            scores = contract_last(keys, qm_ref[side]) + bias
            slopes = contract_last(values, um_ref[side])
            new = jnp.maximum(old, jnp.max(scores, 0, keepdims=True))
            fade = jnp.exp((old - new) * scale)
            expos = jnp.exp((scores - new) * scale)
            result += [
                new,
                total * fade + jnp.sum(expos, 0, keepdims=True),
                weighted * fade + jnp.sum(expos * slopes, 0, keepdims=True),
            ]
        return tuple(result)

    zero = jnp.zeros((1, tokens), jnp.float32)
    start = (zero + masked_fill, zero, zero)
    done = lax.fori_loop(0, frames // tile, step, start + start)
    for side in range(2):
        head = 2 * pair + side
        for kind in range(3):
            out[kind * heads + head : kind * heads + head + 1, :] = done[3 * side + kind]


def exchange_kernel(
    tile, scale, q_ref, u_ref, b_ref, k_ref, v_ref,
    near, far, rel, own_ref, here_ref, peer_ref, back_ref, kt_ref,
    transit, b_near, b_far, bias_ref, qm_ref, um_ref, send, recv_near, recv_y, recv_far,
    stat_send, stat_recv, b_send, b_recv,
):
    me = lax.axis_index("tm")
    count = lax.axis_size("tm")
    frames = k_ref.shape[0]
    heads = own_ref.shape[0] // 3
    place = lax.rem(me, 4)
    odd = lax.rem(me, 2)
    x_peer = me + 1 - 2 * odd
    y_peer = jnp.where(place < 2, me + 2, me - 2)
    far_peer = me - 1 + 2 * odd
    has_far = (far_peer >= 0) & (far_peer < count)
    corner = (place == 0) | (place == 3)
    up = jnp.where(place == 0, me + 4, me - 4)
    down = jnp.where(place == 0, me - 4, me + 4)
    has_up = corner & (up >= 0) & (up < count)
    has_down = corner & (down >= 0) & (down < count)

    barrier = pltpu.get_barrier_semaphore()

    def greet(peer):
        pl.semaphore_signal(
            barrier, inc=1, device_id={"tm": peer}, device_id_type=pl.DeviceIdType.MESH
        )

    greet(x_peer)
    greet(y_peer)
    pl.when(has_far)(lambda: greet(far_peer))
    pl.when(has_up)(lambda: greet(up))
    pl.when(has_down)(lambda: greet(down))
    callers = 2
    for there in (has_far, has_up, has_down):
        callers = callers + jnp.where(there, 1, 0)
    pl.semaphore_wait(barrier, callers)

    def remote(src, dst, send_sem, recv_sem, peer):
        return pltpu.make_async_remote_copy(
            src_ref=src, dst_ref=dst, send_sem=send_sem, recv_sem=recv_sem,
            device_id={"tm": peer}, device_id_type=pl.DeviceIdType.MESH,
        )

    steps = 2 * (q_ref.shape[1] // LANES)

    def part(c):
        return slice((c // 2) * LANES, (c // 2 + 1) * LANES)

    def first(c):
        src = q_ref if c % 2 == 0 else u_ref
        return remote(
            src.at[:, part(c)], near.at[c % 2, :, part(c)], send.at[0, c], recv_near.at[c], x_peer
        )

    def second_final(c):
        return remote(
            near.at[c % 2, :, part(c)], far.at[c % 2, :, part(c)], send.at[1, c], recv_far.at[c], y_peer
        )

    def second_transit(c):
        return remote(
            near.at[c % 2, :, part(c)], transit.at[c % 2, :, part(c)], send.at[1, c], recv_y.at[c], y_peer
        )

    def third(c):
        return remote(
            transit.at[c % 2, :, part(c)], far.at[c % 2, :, part(c)], send.at[2, c], recv_far.at[c], up
        )

    to_near = remote(b_ref, b_near, b_send.at[0], b_recv.at[0], x_peer)
    to_far = remote(b_ref, b_far, b_send.at[1], b_recv.at[1], far_peer)
    to_near.start()
    pl.when(has_far)(lambda: to_far.start())
    for c in range(steps):
        first(c).start()

    @pl.when(jnp.logical_not(has_far))
    def _():
        far[...] = jnp.zeros_like(far)
        b_far[...] = jnp.zeros_like(b_far)
        peer_ref[1] = jnp.zeros_like(own_ref)
        back_ref[1, 0:heads, :] = jnp.full((heads, own_ref.shape[1]), masked_fill, jnp.float32)
        back_ref[1, heads:, :] = jnp.zeros((2 * heads, own_ref.shape[1]), jnp.float32)

    base = me * frames
    rel[0] = b_ref[...] - base
    bias_from(rel.at[0], bias_ref.at[0], tile)
    kt_ref[...] = k_ref[...].T

    own_sends = [
        remote(own_ref, peer_ref.at[0], stat_send.at[0], stat_recv.at[0], x_peer),
        remote(own_ref, peer_ref.at[1], stat_send.at[1], stat_recv.at[1], far_peer),
    ]
    back_sends = [
        remote(here_ref.at[0], back_ref.at[0], stat_send.at[2], stat_recv.at[2], x_peer),
        remote(here_ref.at[1], back_ref.at[1], stat_send.at[3], stat_recv.at[3], far_peer),
    ]

    def own_unit(pair):
        pair_stats(pair, tile, scale, k_ref, v_ref, q_ref, u_ref, bias_ref.at[0], own_ref, qm_ref, um_ref)
        if pair == heads // 2 - 1:
            own_sends[0].start()
            pl.when(has_far)(lambda: own_sends[1].start())

    def near_unit(pair):
        pair_stats(
            pair, tile, scale, k_ref, v_ref, near.at[0], near.at[1], bias_ref.at[1], here_ref.at[0], qm_ref, um_ref
        )
        if pair == heads // 2 - 1:
            back_sends[0].start()

    def far_unit(pair):
        pair_stats(
            pair, tile, scale, k_ref, v_ref, far.at[0], far.at[1], bias_ref.at[2], here_ref.at[1], qm_ref, um_ref
        )

    def need(pair):
        return 2 * ((window_start(pair) + 2 * LANES) // LANES)

    waited_far = [0]
    passed_y = [0]

    def pass_on(upto):
        while passed_y[0] < upto:
            c = passed_y[0]

            @pl.when(corner)
            def _():
                second_transit(c).wait_recv()
                pl.when(has_up)(lambda: third(c).start())

            passed_y[0] += 1

    def far_ready(upto):
        while waited_far[0] < upto:
            c = waited_far[0]
            pl.when(has_far)(lambda: second_final(c).wait_recv())
            waited_far[0] += 1

    pairs = heads // 2
    near_next, own_next, far_next = 0, 0, 0
    for c in range(steps):
        first(c).wait_recv()
        pl.when(corner)(lambda: second_final(c).start())
        pl.when(jnp.logical_not(corner))(lambda: second_transit(c).start())
        pass_on(c - 1)
        if c == 0:
            to_near.wait_recv()
            rel[1] = b_near[...] - base
            bias_from(rel.at[1], bias_ref.at[1], tile)
        if own_next < pairs:
            own_unit(own_next)
            own_next += 1
        elif near_next < pairs and need(near_next) <= c + 1:
            near_unit(near_next)
            near_next += 1
        elif far_next < pairs and need(far_next) <= c - 3:
            if far_next == 0:
                pl.when(has_far)(lambda: to_far.wait_recv())
                rel[2] = b_far[...] - base
                bias_from(rel.at[2], bias_ref.at[2], tile)
            far_ready(need(far_next))
            far_unit(far_next)
            far_next += 1
    while passed_y[0] < steps or near_next < pairs or far_next < pairs:
        pass_on(min(steps, passed_y[0] + 1 if passed_y[0] < steps - 2 else steps))
        if near_next < pairs:
            near_unit(near_next)
            near_next += 1
            continue
        if far_next < pairs:
            if far_next == 0:
                pl.when(has_far)(lambda: to_far.wait_recv())
                rel[2] = b_far[...] - base
                bias_from(rel.at[2], bias_ref.at[2], tile)
            if need(far_next) > steps - 4:
                pass_on(steps)
            far_ready(need(far_next))
            far_unit(far_next)
            far_next += 1
    far_ready(steps)
    pl.when(has_far)(lambda: back_sends[1].start())

    to_near.wait_send()
    pl.when(has_far)(lambda: to_far.wait_send())
    for c in range(steps):
        first(c).wait_send()
        second_final(c).wait_send()
        pl.when(has_up)(lambda: third(c).wait_send())
    own_sends[0].wait()
    back_sends[0].wait()

    @pl.when(has_far)
    def _():
        own_sends[1].wait()
        back_sends[1].wait()


def grads_kernel(offsets, n_stats, tile, scale, k_ref, v_ref, kt_ref, *refs):
    guests = len(offsets)
    inputs = []
    for kinds in n_stats:
        inputs.append(refs[: 3 + kinds])
        refs = refs[3 + kinds :]
    dk_out, dv_out = refs[:2]
    dq_outs = refs[2 : 2 + guests]
    qm_ref, um_ref, bias_ref, norm_ref, dqt_ref, dk_ref, dv_ref = refs[2 + guests :]
    dk_ref[...] = jnp.zeros_like(dk_ref)
    dv_ref[...] = jnp.zeros_like(dv_ref)
    heads, tokens, window = qm_ref.shape
    for guest, offset in enumerate(offsets):
        q_ref, u_ref, b_ref = inputs[guest][:3]
        stats = [r[...] for r in inputs[guest][3:]]
        peak = stats[0][0:heads]
        for one in stats[1:]:
            peak = jnp.maximum(peak, one[0:heads])
        total = jnp.zeros_like(peak)
        weighted = jnp.zeros_like(peak)
        for one in stats:
            factor = jnp.exp((one[0:heads] - peak) * scale)
            total = total + one[heads : 2 * heads] * factor
            weighted = weighted + one[2 * heads :] * factor
        total = jnp.where(total > 0.0, total, 1.0)
        norm_ref[0:heads, :] = peak * scale + jnp.log(total)
        norm_ref[heads:, :] = weighted / total
        mask_heads(q_ref, qm_ref)
        mask_heads(u_ref, um_ref)
        dqt_ref[...] = jnp.zeros_like(dqt_ref)

        def body(low):
            def pair_step(pair, carry):
                cols = pl.ds(pl.multiple_of(window_start(pair), LANES), window)
                keys = k_ref[low : low + tile, cols]
                values = v_ref[low : low + tile, cols]
                inside = bias_ref[low : low + tile, :] == 0.0
                key_term = value_term = None
                for side in range(2):
                    head = 2 * pair + side
                    scores = contract_last(keys, qm_ref[head])
                    slopes = contract_last(values, um_ref[head])
                    log_total = norm_ref[pl.ds(head, 1), :]
                    delta = norm_ref[pl.ds(heads + head, 1), :]
                    probs = jnp.where(inside, jnp.exp(scores * scale - log_total), 0.0)
                    grad = (probs * ((slopes - delta) * scale)).astype(jnp.bfloat16)
                    key_one = mm(grad, qm_ref[head])
                    value_one = mm(probs.astype(jnp.bfloat16), um_ref[head])
                    key_term = key_one if side == 0 else key_term + key_one
                    value_term = value_one if side == 0 else value_term + value_one
                    rows = pl.ds(pl.multiple_of(head * HD, HD // 3), HD)
                    dqt_ref[rows, :] += mm(kt_ref[rows, low : low + tile], grad)
                dk_ref[low : low + tile, cols] += key_term
                dv_ref[low : low + tile, cols] += value_term
                return carry

            lax.fori_loop(0, heads // 2, pair_step, 0)

        frame_tiles(b_ref, bias_ref, offset, tile, body)
        dq_outs[guest][...] = dqt_ref[...].T.astype(dq_outs[guest].dtype)
    dk_out[...] = dk_ref[...].astype(jnp.bfloat16)
    dv_out[...] = dv_ref[...].astype(jnp.bfloat16)


def conv_kernel(block, h_ref, before_ref, after_ref, taps_ref, out_ref, x_ref, w_ref):
    chunks, rows, _ = x_ref.shape
    frames = rows - 2 * HALO
    for chunk in range(chunks):
        cols = slice(chunk * LANES, (chunk + 1) * LANES)
        x_ref[chunk, 0:HALO, :] = before_ref[:, cols].astype(jnp.float32)
        x_ref[chunk, HALO : HALO + frames, :] = h_ref[:, cols].astype(jnp.float32)
        x_ref[chunk, HALO + frames :, :] = after_ref[:, cols].astype(jnp.float32)
        w_ref[chunk, 0:KERNEL, :] = taps_ref[:, cols].astype(jnp.float32)
    for chunk in range(chunks):
        cols = slice(chunk * LANES, (chunk + 1) * LANES)

        def step(index, carry):
            low = pl.multiple_of(index * block, block)
            acc = x_ref[chunk, pl.ds(low + HALO, block), :]
            for tap in range(KERNEL):
                acc = acc + w_ref[chunk, tap : tap + 1, :] * x_ref[
                    chunk, pl.ds(low + HALO + HALF - tap, block), :
                ]
            out_ref[pl.ds(low, block), cols] = acc.astype(jnp.bfloat16)
            return carry

        lax.fori_loop(0, frames // block, step, 0)


def tail_kernel(
    rows, block, kl_ref, vl_ref, near_dq, far_dq, own_dq, taps_ref,
    hidden_hbm, ew_hbm, sw_hbm, kw_hbm, vw_hbm,
    out_ref, query_ref,
    hidden_ref, ew_ref, sw_ref, kw_ref, vw_ref,
    part, part_in, pre, theirs, theirs_in, mine, low_ref, edge, edge_in, terms,
    x_ref, w_ref, load, send, recv, send_part, recv_part, send_back, recv_back,
):
    me = lax.axis_index("tm")
    side = lax.axis_index("mp")
    count = lax.axis_size("tm")
    frames, width = kl_ref.shape
    units = sw_ref.shape[0]
    full = kw_ref.shape[0]
    step_cols = 2 * LANES
    odd = lax.rem(me, 2)
    near_peer = me + 1 - 2 * odd
    far_peer = me - 1 + 2 * odd
    has_far = (far_peer >= 0) & (far_peer < count)
    other = 1 - side

    loads = [
        pltpu.make_async_copy(src, dst, load.at[i])
        for i, (src, dst) in enumerate(
            ((kw_hbm, kw_ref), (vw_hbm, vw_ref), (sw_hbm, sw_ref), (hidden_hbm, hidden_ref), (ew_hbm, ew_ref))
        )
    ]
    for one in loads:
        one.start()

    barrier = pltpu.get_barrier_semaphore()
    mesh = pl.DeviceIdType.MESH
    pl.semaphore_signal(barrier, inc=1, device_id={"mp": other}, device_id_type=mesh)
    pl.semaphore_signal(barrier, inc=1, device_id={"tm": near_peer}, device_id_type=mesh)

    @pl.when(has_far)
    def _():
        pl.semaphore_signal(barrier, inc=1, device_id={"tm": far_peer}, device_id_type=mesh)

    def remote(src, dst, send_sem, recv_sem, peer):
        return pltpu.make_async_remote_copy(
            src_ref=src, dst_ref=dst, send_sem=send_sem, recv_sem=recv_sem,
            device_id=peer, device_id_type=mesh,
        )

    near, far, twin = {"tm": near_peer}, {"tm": far_peer}, {"mp": other}
    query_sends = (
        remote(near_dq, terms.at[0], send.at[0], recv.at[0], near),
        remote(far_dq, terms.at[1], send.at[1], recv.at[1], far),
    )
    near_row = pl.multiple_of(jnp.where(odd == 1, 0, frames - HALO), HALO)
    far_row = pl.multiple_of(jnp.where(odd == 1, frames - HALO, 0), HALO)
    edge_sends = (
        remote(edge.at[0], edge_in.at[0], send.at[2], recv.at[2], near),
        remote(edge.at[1], edge_in.at[1], send.at[3], recv.at[3], far),
    )

    def part_send(piece):
        at = pl.ds(piece * rows, rows)
        return remote(part.at[at], part_in.at[at], send_part.at[piece], recv_part.at[piece], twin)

    def back_send(piece):
        at = pl.ds(piece * rows, rows)
        return remote(theirs.at[at], theirs_in.at[at], send_back.at[piece], recv_back.at[piece], twin)

    chunks = width // LANES
    for chunk in range(chunks):
        cols = slice(chunk * LANES, (chunk + 1) * LANES)
        w_ref[chunk, 0:KERNEL, :] = taps_ref[:, cols].astype(jnp.float32)

    pieces = frames // rows
    order = [0] + ([pieces - 1] if pieces > 1 else []) + list(range(1, pieces - 1))
    loads[0].wait()
    loads[1].wait()
    for number, piece in enumerate(order):
        at = slice(piece * rows, (piece + 1) * rows)

        def encode(index, carry):
            cols = pl.ds(pl.multiple_of(index * step_cols, step_cols), step_cols)
            total = contract_last(kl_ref[at, :], kw_ref[cols, :]) + contract_last(
                vl_ref[at, :], vw_ref[cols, :]
            )
            part[at, cols] = total.astype(jnp.bfloat16)
            return carry

        lax.fori_loop(0, full // step_cols, encode, 0)
        if number == 0:
            callers = 2 + jnp.where(has_far, 1, 0)
            pl.semaphore_wait(barrier, callers)
        part_send(piece).start()
        if number == 0:
            query_sends[0].start()
            pl.when(has_far)(lambda: query_sends[1].start())

    def feed(piece):
        at = slice(piece * rows, (piece + 1) * rows)
        part_send(piece).wait_recv()
        low_ref[...] = (
            part[at, :].astype(jnp.float32) + part_in[at, :].astype(jnp.float32)
        ).astype(jnp.bfloat16)

        def act(index, carry):
            cols = pl.ds(pl.multiple_of(index * step_cols, step_cols), step_cols)
            slope = silu_slope(hidden_ref[at, cols].astype(jnp.float32))
            gain = 0.5 * contract_last(low_ref[...], sw_ref[cols, :])
            pre[:, cols] = (gain * slope).astype(jnp.bfloat16)
            return carry

        lax.fori_loop(0, units // step_cols, act, 0)

        def back(whose, dst):
            def step(index, carry):
                first = pl.multiple_of(index * step_cols, step_cols)
                source = pl.ds(pl.multiple_of(whose * width + first, step_cols), step_cols)
                dst[at, pl.ds(first, step_cols)] = contract_last(
                    pre[...], ew_ref[source, :]
                ).astype(jnp.bfloat16)
                return carry

            lax.fori_loop(0, width // step_cols, step, 0)

        back(other, theirs)
        back_send(piece).start()
        back(side, mine)

    def finish(piece):
        at = slice(piece * rows, (piece + 1) * rows)
        back_send(piece).wait_recv()

        def step(chunk, carry):
            cols = pl.ds(pl.multiple_of(chunk * LANES, LANES), LANES)
            own = pl.ds(pl.multiple_of(side * width + chunk * LANES, LANES), LANES)
            total = part[at, own].astype(jnp.float32) + part_in[at, own].astype(jnp.float32)
            back = mine[at, cols].astype(jnp.float32) + theirs_in[at, cols].astype(jnp.float32)
            low = (total + back).astype(jnp.bfloat16)
            mine[at, cols] = low
            x_ref[chunk, HALO + piece * rows : HALO + (piece + 1) * rows, :] = low.astype(jnp.float32)
            return carry

        lax.fori_loop(0, chunks, step, 0)

    def send_edges():
        edge[0] = mine[pl.ds(near_row, HALO), :]
        edge[1] = mine[pl.ds(far_row, HALO), :]
        edge_sends[0].start()
        pl.when(has_far)(lambda: edge_sends[1].start())

    loads[2].wait()
    loads[3].wait()
    loads[4].wait()
    for number, piece in enumerate(order):
        feed(piece)
        if number >= 1:
            finish(order[number - 1])
        if number == 2:
            send_edges()
    finish(order[-1])
    if len(order) < 3:
        send_edges()

    def conv(chunk, low):
        acc = x_ref[chunk, pl.ds(low + HALO, block), :]
        for tap in range(KERNEL):
            acc = acc + w_ref[chunk, tap : tap + 1, :] * x_ref[
                chunk, pl.ds(low + HALO + HALF - tap, block), :
            ]
        cols = pl.ds(pl.multiple_of(chunk * LANES, LANES), LANES)
        out_ref[pl.ds(low, block), cols] = acc.astype(jnp.bfloat16)

    blocks = frames // block

    def inner(index, carry):
        conv(index // (blocks - 2), pl.multiple_of((1 + index % (blocks - 2)) * block, block))
        return carry

    lax.fori_loop(0, chunks * (blocks - 2), inner, 0)

    edge_sends[0].wait()

    @pl.when(has_far)
    def _():
        edge_sends[1].wait()

    @pl.when(jnp.logical_not(has_far))
    def _():
        edge_in[1] = jnp.zeros((HALO, width), jnp.bfloat16)
        terms[1] = jnp.zeros((terms.shape[1], width), jnp.bfloat16)

    near_at = pl.multiple_of(jnp.where(odd == 1, 0, frames + HALO), HALO)
    far_at = pl.multiple_of(jnp.where(odd == 1, frames + HALO, 0), HALO)
    for chunk in range(chunks):
        cols = slice(chunk * LANES, (chunk + 1) * LANES)
        x_ref[chunk, pl.ds(near_at, HALO), :] = edge_in[0, :, cols].astype(jnp.float32)
        x_ref[chunk, pl.ds(far_at, HALO), :] = edge_in[1, :, cols].astype(jnp.float32)

    def outer(index, carry):
        conv(index // 2, pl.multiple_of((index % 2) * (blocks - 1) * block, block))
        return carry

    lax.fori_loop(0, chunks * 2, outer, 0)

    query_sends[0].wait()
    pl.when(has_far)(lambda: query_sends[1].wait())
    query_ref[...] = (
        own_dq[...] + terms[0].astype(jnp.float32) + terms[1].astype(jnp.float32)
    ).astype(jnp.bfloat16)
    for piece in order:
        part_send(piece).wait_send()
        back_send(piece).wait_send()


def tail(
    key_low, value_low, near_dq, far_dq, own_dq,
    hidden_pre, expand_weight, shrink_weight, key_weight, value_weight, kernel_taps,
):
    frames, width = key_low.shape
    tokens = own_dq.shape[0]
    full, units = key_weight.shape[0], shrink_weight.shape[0]
    rows = tile_of(frames)
    pieces = frames // rows
    bf16, f32 = jnp.bfloat16, jnp.float32
    chunks = width // LANES
    dma = pltpu.SemaphoreType.DMA
    weights = (hidden_pre, expand_weight, shrink_weight, key_weight, value_weight)
    return pl.pallas_call(
        functools.partial(tail_kernel, rows, rows // 4),
        out_shape=[
            jax.ShapeDtypeStruct((frames, width), bf16),
            jax.ShapeDtypeStruct((tokens, width), bf16),
        ],
        in_specs=[VMEM] * 6 + [pl.BlockSpec(memory_space=pl.ANY)] * 5,
        out_specs=[VMEM] * 2,
        scratch_shapes=[pltpu.VMEM(w.shape, bf16) for w in weights]
        + [
            pltpu.VMEM((frames, full), bf16),
            pltpu.VMEM((frames, full), bf16),
            pltpu.VMEM((rows, units), bf16),
            pltpu.VMEM((frames, width), bf16),
            pltpu.VMEM((frames, width), bf16),
            pltpu.VMEM((frames, width), bf16),
            pltpu.VMEM((rows, full), bf16),
            pltpu.VMEM((2, HALO, width), bf16),
            pltpu.VMEM((2, HALO, width), bf16),
            pltpu.VMEM((2, tokens, width), bf16),
            pltpu.VMEM((chunks, frames + 2 * HALO, LANES), f32),
            pltpu.VMEM((chunks, KERNEL + 1, LANES), f32),
            dma((5,)), dma((4,)), dma((4,)),
            dma((pieces,)), dma((pieces,)), dma((pieces,)), dma((pieces,)),
        ],
        compiler_params=pltpu.CompilerParams(
            collective_id=1, has_side_effects=True, vmem_limit_bytes=44 << 20
        ),
        name="tail",
    )(key_low, value_low, near_dq, far_dq, own_dq, kernel_taps, *weights)


def tile_of(frames):
    for tile in (256, 128, 64, 32, 16):
        if frames % tile == 0:
            return tile
    return frames


def params(mib=None):
    return pltpu.CompilerParams(vmem_limit_bytes=None if mib is None else mib << 20)


def relayed(tokens, width):
    groups = lax.axis_size("tm") % 4 == 0
    return groups and lax.axis_size("mp") == 2 and width % 384 == 0 and tokens % LANES == 0


def attention(queries, upstream, bounds, frame_keys, frame_values):
    frames, width = frame_keys.shape
    tokens = queries.shape[0]
    heads = width // HD
    window = window_of(width)
    scale = 1.0 / math.sqrt(HD)
    tile = tile_of(frames)
    f32, bf16 = jnp.float32, jnp.bfloat16
    shape = jax.ShapeDtypeStruct
    masks = [
        pltpu.VMEM((heads, tokens, window), bf16),
        pltpu.VMEM((heads, tokens, window), bf16),
        pltpu.VMEM((frames, tokens), f32),
    ]
    stat = shape((3 * heads, tokens), f32)
    work = 2 * tokens * frames * width
    peers = lax.axis_size("tm")

    def grads(keys_t, offsets, guests):
        n_stats = tuple(len(guest) - 3 for guest in guests)
        arrays = [x for guest in guests for x in guest]
        return pl.pallas_call(
            functools.partial(grads_kernel, offsets, n_stats, tile, scale),
            out_shape=[shape((frames, width), bf16)] * 2
            + [shape((tokens, width), bf16)] * 2
            + [shape((tokens, width), f32)],
            in_specs=[VMEM] * (3 + len(arrays)),
            out_specs=[VMEM] * 5,
            scratch_shapes=masks
            + [pltpu.VMEM((2 * heads, tokens), f32), pltpu.VMEM((width, tokens), f32)]
            + [pltpu.VMEM((frames, width), f32)] * 2,
            compiler_params=params(40),
            cost_estimate=pl.CostEstimate(
                flops=30 * work, bytes_accessed=20 * frames * width, transcendentals=0
            ),
            name="grads",
        )(frame_keys, frame_values, keys_t, *arrays)

    if relayed(tokens, width):
        wide = shape((2, tokens, width), bf16)
        steps = 2 * (width // LANES)
        dma = pltpu.SemaphoreType.DMA
        near, far, rel, own_stats, here, peer, back, keys_t = pl.pallas_call(
            functools.partial(exchange_kernel, tile, scale),
            out_shape=[wide, wide, shape((3, 2, tokens), jnp.int32), stat]
            + [shape((2, 3 * heads, tokens), f32)] * 3
            + [shape((width, frames), bf16)],
            in_specs=[VMEM] * 5,
            out_specs=[VMEM] * 8,
            scratch_shapes=[
                pltpu.VMEM((2, tokens, width), bf16),
                pltpu.VMEM((2, tokens), jnp.int32),
                pltpu.VMEM((2, tokens), jnp.int32),
                pltpu.VMEM((3, frames, tokens), f32),
                pltpu.VMEM((2, tokens, window), bf16),
                pltpu.VMEM((2, tokens, window), bf16),
                dma((3, steps)), dma((steps,)), dma((steps,)), dma((steps,)),
                dma((4,)), dma((4,)), dma((2,)), dma((2,)),
            ],
            compiler_params=pltpu.CompilerParams(
                collective_id=0, has_side_effects=True, vmem_limit_bytes=32 << 20
            ),
            name="exchange",
        )(queries, upstream, bounds.T, frame_keys, frame_values)
        key_low, value_low, near_dq, far_dq, own_dq = grads(
            keys_t,
            (0, 0, 0),
            (
                (near[0], near[1], rel[1], here[0], peer[0]),
                (far[0], far[1], rel[2], here[1], peer[1]),
                (queries, upstream, rel[0], own_stats, back[0], back[1]),
            ),
        )
        return key_low, value_low, near_dq, far_dq, own_dq
    else:
        base = lax.axis_index("tm") * frames
        own = (queries, upstream, (bounds - base).T)
        prev = tuple(shifted(x, "tm", 1) for x in own)
        after = tuple(shifted(x, "tm", -1) for x in own)

        def stats(offsets, guests):
            return pl.pallas_call(
                functools.partial(stats_kernel, offsets, tile, scale),
                out_shape=[stat] * len(offsets),
                in_specs=[VMEM] * (2 + 3 * len(offsets)),
                out_specs=[VMEM] * len(offsets),
                scratch_shapes=masks,
                compiler_params=params(24),
                name="stats%d" % len(offsets),
            )(frame_keys, frame_values, *[x for guest in guests for x in guest])

        (own_stats,) = stats((0,), (own,))
        prev_own = shifted(own_stats, "tm", 1)
        after_own = shifted(own_stats, "tm", -1)
        prev_stats, after_stats = stats((-frames, frames), (prev, after))
        from_after = shifted(prev_stats, "tm", -1)
        from_prev = shifted(after_stats, "tm", 1)
        position = lax.axis_index("tm")
        empty = jnp.where(jnp.arange(3 * heads) < heads, masked_fill, 0.0).astype(f32)[:, None]
        from_prev = jnp.where(position == 0, empty, from_prev)
        from_after = jnp.where(position == peers - 1, empty, from_after)
        key_low, value_low, prev_dq, after_dq, own_dq = grads(
            frame_keys.T,
            (-frames, frames, 0),
            (
                (*prev, prev_stats, prev_own),
                (*after, after_stats, after_own),
                (*own, own_stats, from_prev, from_after),
            ),
        )
        terms = (shifted(prev_dq, "tm", -1), shifted(after_dq, "tm", 1))
    query_gradient = own_dq + terms[0].astype(f32) + terms[1].astype(f32)
    return key_low, value_low, query_gradient.astype(bf16)


def depthwise(hidden_gradient, kernel_taps):
    frames, width = hidden_gradient.shape
    before = shifted(hidden_gradient[frames - HALO :], "tm", 1)
    after = shifted(hidden_gradient[:HALO], "tm", -1)
    chunks = width // LANES
    return pl.pallas_call(
        functools.partial(conv_kernel, tile_of(frames) // 4),
        out_shape=jax.ShapeDtypeStruct((frames, width), jnp.bfloat16),
        in_specs=[VMEM] * 4,
        out_specs=VMEM,
        scratch_shapes=[
            pltpu.VMEM((chunks, frames + 2 * HALO, LANES), jnp.float32),
            pltpu.VMEM((chunks, KERNEL + 1, LANES), jnp.float32),
        ],
        compiler_params=params(16),
        name="conv",
    )(hidden_gradient, before, after, kernel_taps)


def plain_depthwise(hidden_gradient, kernel_taps):
    frames = hidden_gradient.shape[0]
    before = shifted(hidden_gradient[frames - HALF :], "tm", 1)
    after = shifted(hidden_gradient[:HALF], "tm", -1)
    padded = jnp.concatenate([before, hidden_gradient, after], 0).astype(jnp.float32)
    weights = kernel_taps.astype(jnp.float32)
    result = hidden_gradient.astype(jnp.float32)
    for tap in range(KERNEL):
        lower = 2 * HALF - tap
        result = result + weights[tap] * padded[lower : lower + frames]
    return result.astype(jnp.bfloat16)


def mp_sum(part):
    if lax.axis_size("mp") == 2:
        other = lax.ppermute(part, "mp", [(0, 1), (1, 0)])
        return part.astype(jnp.float32) + other.astype(jnp.float32)
    return lax.psum(part, "mp").astype(jnp.float32)


def mp_scatter(part, width):
    me = lax.axis_index("mp")
    if lax.axis_size("mp") == 2:
        mine = lax.dynamic_slice_in_dim(part, me * width, width, 1)
        theirs = lax.dynamic_slice_in_dim(part, (1 - me) * width, width, 1)
        other = lax.ppermute(theirs, "mp", [(0, 1), (1, 0)])
        return mine.astype(jnp.float32) + other.astype(jnp.float32)
    return lax.psum_scatter(part, "mp", scatter_dimension=1, tiled=True).astype(jnp.float32)


def feed_forward(key_low, value_low, hidden_pre, expand_weight, shrink_weight, key_weight, value_weight):
    frames, width = key_low.shape
    pieces = 2 if frames % 32 == 0 else 1
    size = frames // pieces
    me = lax.axis_index("mp")
    sums = []
    for piece in range(pieces):
        rows = slice(piece * size, (piece + 1) * size)
        part = contract_last(key_low[rows], key_weight) + contract_last(value_low[rows], value_weight)
        sums.append(mp_sum(part.astype(jnp.bfloat16)))
    out = []
    for piece in range(pieces):
        rows = slice(piece * size, (piece + 1) * size)
        act = 0.5 * contract_last(sums[piece].astype(jnp.bfloat16), shrink_weight)
        pre = (act * silu_slope(hidden_pre[rows].astype(jnp.float32))).astype(jnp.bfloat16)
        back = mp_scatter(contract_last(pre, expand_weight).astype(jnp.bfloat16), width)
        mine = lax.dynamic_slice_in_dim(sums[piece], me * width, width, 1)
        out.append((mine + back).astype(jnp.bfloat16))
    return jnp.concatenate(out, 0) if pieces > 1 else out[0]


def shards(
    queries,
    upstream,
    bounds,
    frame_keys,
    frame_values,
    hidden_pre,
    expand_weight,
    shrink_weight,
    key_weight,
    value_weight,
    kernel_taps,
):
    found = attention(queries, upstream, bounds, frame_keys, frame_values)
    if relayed(queries.shape[0], queries.shape[1]):
        return tail(
            *found, hidden_pre, expand_weight, shrink_weight, key_weight, value_weight, kernel_taps
        )
    key_low, value_low, query_gradient = found
    hidden_gradient = feed_forward(
        key_low, value_low, hidden_pre, expand_weight, shrink_weight, key_weight, value_weight
    )
    if hidden_gradient.shape[1] % LANES == 0:
        frame_gradient = depthwise(hidden_gradient, kernel_taps)
    else:
        frame_gradient = plain_depthwise(hidden_gradient, kernel_taps)
    return (frame_gradient, query_gradient)


def solution(mesh):
    placed = (
        P("tm", "mp"),
        P("tm", "mp"),
        P("tm", None),
        P("tm", "mp"),
        P("tm", "mp"),
        P("tm", "mp"),
        P(None, "mp"),
        P("mp", None),
        P(None, "mp"),
        P(None, "mp"),
        P(None, "mp"),
    )
    return jax.shard_map(
        shards,
        mesh=mesh,
        in_specs=placed,
        out_specs=(P("tm", "mp"), P("tm", "mp")),
        check_vma=False,
    )
```
